512 devices in a mesh: dp: 16 (over y, x), seq: 32 (over z, core).
Axes of the slice: x: 4, y: 4, z: 16, core: 2. Of those that a mesh axis runs over, the one named last changes fastest.
Arguments:
- queries: bfloat16 [65536, 32, 128], P(('dp', 'seq')), parts along dimension 0, may hold values from -6 to 6
- attn_keys: bfloat16 [65536, 32, 128], P(('dp', 'seq')), parts along dimension 0, may hold values from -6 to 6
- attn_values: bfloat16 [65536, 32, 128], P(('dp', 'seq')), parts along dimension 0, may hold values from -6 to 6
- splats: bfloat16 [16384, 32, 128], P(('dp', 'seq')), parts along dimension 0, may hold values from -6 to 6
- splat_dest: int32 [16384], P(('dp', 'seq')), parts along dimension 0, may hold values from 0 to 31, as said below
- splat_sub: int32 [16384], P(('dp', 'seq')), parts along dimension 0, may hold values from 0 to 3
- splat_weight: bfloat16 [16384], P(('dp', 'seq')), parts along dimension 0, may hold values from 0.049804688 to 0.5
- cond_weight: bfloat16 [128, 32, 128], P(None, 'seq'), may hold values from -0.5 to 0.5
Outputs:
- attn_out: bfloat16 [65536, 32, 128], P(('dp', 'seq')), parts along dimension 0
The draws below stay inside these ranges and needn't reach their ends.
There are 16 independent parts, one for each index of `dp`. The reference program is written for one: setup_inputs(seed, part) draws one part's arguments, and reference() takes and returns one part's arrays. A program takes and returns all parts, laid end to end along the dimension named above; an argument that names none is the same for every part. Nothing has to cross between parts.
Inputs may be any that keep to these rules, and one draw needn't show every extreme that they name: `splat_dest`: of the splat blocks that one device holds, at most 2 name the same device; one device, drawn afresh, is named by exactly 2 splat blocks of every device.
All inputs are finite; a program needn't handle non-finite values.
Results may differ from the reference program's by a relative error of at most 0.0059.
Values may be sent and summed in bfloat16 or wider, within the bound.
No kernel may reach another device: no remote copies, remote signals or barrier semaphores. Data moves between devices by JAX's collectives and lax.ppermute only.
A program may use at most 64 MiB of HBM per device.

```python
import math
import jax
import jax.numpy as jnp
from jax import lax

HD = 128
HEADS = 32
CF = 128
BT = 32
SPL_DEV = 32
NTB = 4
SEQ = 4096
NSPL = 1024
CAP = 2
N_SEQ = 32


def base_field(key):
    return jnp.clip(1.6 * jax.random.normal(key, (SEQ, HEADS, HD), jnp.float32), -6.0, 6.0)


def draw_queries(key, part):
    field = base_field(jax.random.fold_in(key, 41))
    return field.astype(jnp.bfloat16)


def draw_attn_keys(key, part):
    field = base_field(jax.random.fold_in(key, 51))
    return field.astype(jnp.bfloat16)


def draw_splat_dest(key, part):
    hot_dest = jax.random.randint(jax.random.fold_in(key, 11), (), 0, N_SEQ)
    device_keys = jax.random.split(jax.random.fold_in(key, 12), N_SEQ)
    pool_size = (N_SEQ - 1) * CAP

    def per_device(device_key):
        first_key, second_key = jax.random.split(device_key)
        chosen = jax.random.permutation(first_key, pool_size)[:SPL_DEV - CAP]
        destinations = (chosen // CAP).astype(jnp.int32)
        destinations = destinations + (destinations >= hot_dest).astype(jnp.int32)
        dest_rows = jnp.concatenate([jnp.full((CAP,), hot_dest, jnp.int32), destinations])
        shuffle = jax.random.permutation(second_key, SPL_DEV)
        return dest_rows[shuffle]
    return jax.vmap(per_device)(device_keys).reshape(-1).astype(jnp.int32)


def with_ends(array, key, low, high):
    spot = [jax.random.randint(jax.random.fold_in(key, axis), (), 0, length) for axis, length in enumerate(array.shape)]
    longest = array.shape.index(max(array.shape))
    beside = spot[:longest] + [(spot[longest] + 1) % array.shape[longest]] + spot[longest + 1:]
    return array.at[tuple(spot)].set(low).at[tuple(beside)].set(high)


def block_scale(own_key, shape, cuts, low, largest):
    level, own = 1.0, jax.random.fold_in(own_key, 6)
    for axis_at, parts in cuts:
        heights = jnp.exp(jax.random.uniform(jax.random.fold_in(own, axis_at), (parts,), jnp.float32, low / len(cuts), largest / len(cuts)))
        level = level * jnp.repeat(heights, shape[axis_at] // parts).reshape([-1 if axis == axis_at else 1 for axis in range(len(shape))])
    return level


def noise(stream_key, dims, scale, limit, cuts=(), held_as=jnp.bfloat16):
    entries = scale * jax.random.normal(stream_key, dims, jnp.float32)
    if cuts:
        entries = entries * block_scale(stream_key, dims, cuts, -0.22, 0.18)
    return jnp.clip(entries, -limit, limit).astype(held_as)


def setup_inputs(seed: int = 0, part: int = 0) -> dict:
    keys = jax.random.split(jax.random.key(seed), 9)
    part_keys = jax.random.split(jax.random.fold_in(keys[8], part), 9)
    return {
        "queries": draw_queries(jax.random.fold_in(jax.random.fold_in(keys[8], part), 71), part),
        "attn_keys": draw_attn_keys(jax.random.fold_in(jax.random.fold_in(keys[8], part), 71), part),
        "attn_values": noise(part_keys[2], (SEQ, HEADS, HD), 1.0, 6.0, ((0, 32),)),
        "splats": noise(part_keys[3], (NSPL, BT, CF), 1.0, 6.0, ((0, 32),)),
        "splat_dest": draw_splat_dest(jax.random.fold_in(jax.random.fold_in(keys[8], part), 71), part),
        "splat_sub": with_ends(jax.random.randint(part_keys[5], (NSPL,), 0, NTB), jax.random.fold_in(part_keys[5], 1), 0, NTB - 1).astype(jnp.int32),
        "splat_weight": jnp.clip(jnp.exp(math.log(0.5) - 2.306499 * jax.random.uniform(part_keys[6], (NSPL,), jnp.float32) ** block_scale(part_keys[6], (NSPL,), ((0, 32),), -0.2, 0.2)), 0.049804688, 0.5).astype(jnp.bfloat16),
        "cond_weight": noise(keys[7], (CF, HEADS, HD), CF ** -0.5, 0.5, ((1, 32),)),
    }


def normalize(block_sums, block_weights, feats):
    denom = jnp.maximum(block_weights, 1.0)
    return (block_sums / denom[:, None]).reshape(-1, feats).astype(jnp.bfloat16)


def reference(queries, attn_keys, attn_values, splats, splat_dest, splat_sub, splat_weight, cond_weight):
    blocks = SEQ // BT
    target = (splat_dest * NTB + splat_sub).astype(jnp.int32)
    block_ids = jnp.arange(blocks, dtype=jnp.int32)
    weight_table = jnp.where(target[None, :] == block_ids[:, None], splat_weight[None, :], jnp.zeros((), jnp.bfloat16))
    splat_rows = splats.reshape(NSPL, BT * CF)
    cond_sum = jnp.dot(weight_table, splat_rows, preferred_element_type=jnp.float32)
    weight_sum = jnp.sum(weight_table.astype(jnp.float32), axis=1)
    cond = normalize(cond_sum, weight_sum, CF)
    cond_mix = jnp.einsum("tc,chd->thd", cond.astype(jnp.float32), cond_weight.astype(jnp.float32))
    mixed_values = (attn_values.astype(jnp.float32) + cond_mix).astype(jnp.bfloat16)
    score_scale = float(HD) ** -0.5

    def one_head(operands):
        query_head, key_head, value_head = operands
        scores = jnp.dot(query_head, key_head.T, preferred_element_type=jnp.float32) * score_scale
        probs = jax.nn.softmax(scores, axis=-1).astype(jnp.bfloat16)
        return jnp.dot(probs, value_head, preferred_element_type=jnp.float32).astype(jnp.bfloat16)

    result = lax.map(one_head, (queries.transpose(1, 0, 2), attn_keys.transpose(1, 0, 2), mixed_values.transpose(1, 0, 2)))
    return result.transpose(1, 0, 2)
```

```python
import math

import jax
import jax.numpy as jnp
from jax import lax
from jax.experimental import pallas as pl
from jax.experimental.pallas import tpu as pltpu
from jax.sharding import PartitionSpec as P


def attention(recv, mix, sub_rows):
    peers, _, rows, hd = recv.shape
    tokens = peers * rows
    tile = 1024
    to_exp2 = hd**-0.5 * math.log2(math.e)

    def kernel(q_ref, k_ref, v_ref, mix_ref, o_ref, v_ext):
        @pl.when(pl.program_id(0) == 0)
        def _():
            values = v_ref[...].reshape(tokens, hd).astype(jnp.float32)
            v_ext[:, :hd] = (values + mix_ref[...]).astype(jnp.bfloat16)
            v_ext[:, hd:] = jnp.ones((tokens, hd), jnp.bfloat16)

        keys = k_ref[...].reshape(tokens, hd)
        for at in range(tile // sub_rows):
            q = q_ref[(at * sub_rows) // rows, 0, pl.ds((at * sub_rows) % rows, sub_rows)]
            scores = lax.dot_general(
                q, keys, (((1,), (1,)), ((), ())), preferred_element_type=jnp.float32
            )
            top = jnp.max(scores, axis=1, keepdims=True)
            probs = jnp.exp2((scores - top) * to_exp2).astype(jnp.bfloat16)
            both = jnp.dot(probs, v_ext[...], preferred_element_type=jnp.float32)
            o_ref[pl.ds(at * sub_rows, sub_rows)] = (both[:, :hd] / both[:, hd:]).astype(
                jnp.bfloat16
            )

    def whole(part):
        return pl.BlockSpec((peers, 1, rows, hd), lambda i: (0, part, 0, 0))

    return pl.pallas_call(
        kernel,
        name="attend",
        grid=(tokens // tile,),
        in_specs=[
            pl.BlockSpec((tile // rows, 1, rows, hd), lambda i: (i, 0, 0, 0)),
            whole(1),
            whole(2),
            pl.BlockSpec((tokens, hd), lambda i: (0, 0)),
        ],
        out_specs=pl.BlockSpec((tile, hd), lambda i: (i, 0)),
        out_shape=jax.ShapeDtypeStruct((tokens, hd), jnp.bfloat16),
        scratch_shapes=[pltpu.VMEM((tokens, 2 * hd), jnp.bfloat16)],
        compiler_params=pltpu.CompilerParams(vmem_limit_bytes=48 << 20),
    )(recv, recv, recv, mix)


def gathered_condition(splats, splat_dest, splat_sub, splat_weight, own_blocks):
    peers = lax.axis_size("seq")
    chips = peers // 2
    count, blk_rows, feats = splats.shape
    blocks = peers * own_blocks
    half = blk_rows // 2
    core = lax.axis_index("seq") % 2
    target = splat_dest * own_blocks + splat_sub
    table = jnp.where(
        target[None, :] == jnp.arange(blocks, dtype=jnp.int32)[:, None],
        splat_weight[None, :],
        jnp.zeros((), jnp.bfloat16),
    )
    halves = splats.reshape(count, 2, half * feats)
    mine = lax.dynamic_index_in_dim(halves, core, 1, keepdims=False)
    other = lax.dynamic_index_in_dim(halves, 1 - core, 1, keepdims=False)
    swap = [(d, d ^ 1) for d in range(peers)]
    arrived = lax.ppermute(jnp.concatenate([other, table.T], axis=1), "seq", swap)
    rows = jnp.concatenate([mine, arrived[:, : half * feats]], axis=0)
    both_table = jnp.concatenate([table, arrived[:, half * feats :].T], axis=1)
    sums = jnp.dot(both_table, rows, preferred_element_type=jnp.float32)
    weights = jnp.sum(both_table.astype(jnp.float32), axis=1, keepdims=True)
    per_chip = 2 * own_blocks
    partial = jnp.concatenate([sums, jnp.broadcast_to(weights, (blocks, 2 * feats))], axis=1)
    same_core = [[2 * z + c for z in range(chips)] for c in range(2)]
    total = lax.psum_scatter(
        partial, "seq", scatter_dimension=0, tiled=True, axis_index_groups=same_core
    )
    denom = jnp.maximum(total[:, half * feats : half * feats + 1], 1.0)
    cond = (total[:, : half * feats] / denom).astype(jnp.bfloat16)
    cond = cond.reshape(per_chip * half, feats)
    everyone = lax.all_gather(cond, "seq", axis=0, tiled=True)
    everyone = everyone.reshape(chips, 2, per_chip, half, feats).transpose(0, 2, 1, 3, 4)
    return everyone.reshape(blocks * blk_rows, feats)


def on_device(
    queries, attn_keys, attn_values, splats, splat_dest, splat_sub, splat_weight, cond_weight
):
    tok_rows, head_count, head_size = queries.shape
    peers = lax.axis_size("seq")
    own_blocks = tok_rows // splats.shape[1]
    send = jnp.concatenate(
        [x.transpose(1, 0, 2) for x in (queries, attn_keys, attn_values)], axis=1
    )
    recv = lax.all_to_all(send, "seq", split_axis=0, concat_axis=0, tiled=True)
    cond = gathered_condition(splats, splat_dest, splat_sub, splat_weight, own_blocks)
    mix = jnp.dot(cond, cond_weight[:, 0], preferred_element_type=jnp.float32)
    head_out = attention(recv.reshape(peers, 3, tok_rows, head_size), mix, 128)
    head_out = head_out.reshape(peers, tok_rows, head_size)
    arrived = lax.all_to_all(head_out, "seq", split_axis=0, concat_axis=0, tiled=True)
    return arrived.transpose(1, 0, 2)


def solution(mesh):
    in_specs = (
        P(("dp", "seq"), None, None),
        P(("dp", "seq"), None, None),
        P(("dp", "seq"), None, None),
        P(("dp", "seq"), None, None),
        P(("dp", "seq")),
        P(("dp", "seq")),
        P(("dp", "seq")),
        P(None, "seq", None),
    )
    out_specs = P(("dp", "seq"), None, None)
    return jax.shard_map(
        on_device, mesh=mesh, in_specs=in_specs, out_specs=out_specs, check_vma=False
    )
```

```python
import math

import jax
import jax.numpy as jnp
from jax import lax
from jax.experimental import pallas as pl
from jax.experimental.pallas import tpu as pltpu
from jax.sharding import PartitionSpec as P


def attention_probs(recv, tile, sub_rows):
    peers, _, rows, hd = recv.shape
    tokens = peers * rows
    to_exp2 = hd**-0.5 * math.log2(math.e)

    def kernel(q_ref, k_ref, p_ref):
        keys = k_ref[...].reshape(tokens, hd)
        for at in range(tile // sub_rows):
            q = q_ref[(at * sub_rows) // rows, 0, pl.ds((at * sub_rows) % rows, sub_rows)]
            scores = lax.dot_general(
                q, keys, (((1,), (1,)), ((), ())), preferred_element_type=jnp.float32
            )
            top = jnp.max(scores, axis=1, keepdims=True)
            probs = jnp.exp2((scores - top) * to_exp2)
            total = jnp.sum(probs, axis=1, keepdims=True)
            p_ref[pl.ds(at * sub_rows, sub_rows)] = (probs * (1.0 / total)).astype(jnp.bfloat16)

    return pl.pallas_call(
        kernel,
        name="probs",
        grid=(tokens // tile,),
        in_specs=[
            pl.BlockSpec((tile // rows, 1, rows, hd), lambda i: (i, 0, 0, 0)),
            pl.BlockSpec((peers, 1, rows, hd), lambda i: (0, 1, 0, 0)),
        ],
        out_specs=pl.BlockSpec((tile, tokens), lambda i: (i, 0)),
        out_shape=jax.ShapeDtypeStruct((tokens, tokens), jnp.bfloat16),
        cost_estimate=pl.CostEstimate(
            flops=2 * tokens * tokens * hd,
            transcendentals=tokens * tokens,
            bytes_accessed=2 * tokens * tokens,
        ),
        compiler_params=pltpu.CompilerParams(vmem_limit_bytes=48 << 20),
    )(recv, recv)


def weigh_values(probs, recv, mix, tile):
    peers, rows, hd = recv.shape
    tokens = peers * rows

    def kernel(p_ref, v_ref, mix_ref, o_ref, mixed):
        @pl.when(pl.program_id(0) == 0)
        def _():
            values = v_ref[...].reshape(tokens, hd).astype(jnp.float32)
            mixed[...] = (values + mix_ref[...]).astype(jnp.bfloat16)

        o_ref[...] = jnp.dot(
            p_ref[...], mixed[...], preferred_element_type=jnp.float32
        ).astype(jnp.bfloat16)

    return pl.pallas_call(
        kernel,
        name="weigh",
        grid=(tokens // tile,),
        in_specs=[
            pl.BlockSpec((tile, tokens), lambda i: (i, 0)),
            pl.BlockSpec((peers, rows, hd), lambda i: (0, 0, 0)),
            pl.BlockSpec((tokens, hd), lambda i: (0, 0)),
        ],
        out_specs=pl.BlockSpec((tile, hd), lambda i: (i, 0)),
        out_shape=jax.ShapeDtypeStruct((tokens, hd), jnp.bfloat16),
        scratch_shapes=[pltpu.VMEM((tokens, hd), jnp.bfloat16)],
        compiler_params=pltpu.CompilerParams(vmem_limit_bytes=48 << 20),
    )(probs, recv, mix)


def gathered_condition(splats, splat_dest, splat_sub, splat_weight, own_blocks):
    peers = lax.axis_size("seq")
    chips = peers // 2
    count, blk_rows, feats = splats.shape
    blocks = peers * own_blocks
    per_chip = 2 * own_blocks
    half = blk_rows // 2
    first_core = lax.axis_index("seq") % 2 == 0
    swap = [(d, d ^ 1) for d in range(peers)]
    same_core = [[2 * z + c for z in range(chips)] for c in range(2)]
    target = splat_dest * own_blocks + splat_sub
    table = jnp.where(
        target[None, :] == jnp.arange(blocks, dtype=jnp.int32)[:, None],
        splat_weight[None, :],
        jnp.zeros((), jnp.bfloat16),
    )
    low = splats[:, :half].reshape(count, half * feats)
    high = splats[:, half:].reshape(count, half * feats)
    mine = jnp.where(first_core, low, high)
    other = jnp.where(first_core, high, low)
    arrived = lax.ppermute(jnp.concatenate([other, table.T], axis=1), "seq", swap)
    rows = jnp.concatenate([mine, arrived[:, : half * feats]], axis=0)
    both_table = jnp.concatenate([table, arrived[:, half * feats :].T], axis=1)
    sums = jnp.dot(both_table, rows, preferred_element_type=jnp.float32)
    weights = jnp.sum(both_table.astype(jnp.float32), axis=1, keepdims=True)
    partial = jnp.concatenate([sums, jnp.broadcast_to(weights, (blocks, 2 * feats))], axis=1)
    total = lax.psum_scatter(
        partial, "seq", scatter_dimension=0, tiled=True, axis_index_groups=same_core
    )
    denom = jnp.maximum(total[:, half * feats : half * feats + 1], 1.0)
    cond = (total[:, : half * feats] / denom).astype(jnp.bfloat16)
    cond = cond.reshape(per_chip, half, feats)
    theirs = lax.ppermute(cond, "seq", swap)
    on_chip = jnp.concatenate(
        [jnp.where(first_core, cond, theirs), jnp.where(first_core, theirs, cond)], axis=1
    )
    on_chip = on_chip.reshape(per_chip * blk_rows, feats)
    return lax.all_gather(on_chip, "seq", axis=0, tiled=True, axis_index_groups=same_core)


def on_device(
    queries, attn_keys, attn_values, splats, splat_dest, splat_sub, splat_weight, cond_weight
):
    tok_rows, head_count, head_size = queries.shape
    peers = lax.axis_size("seq")
    own_blocks = tok_rows // splats.shape[1]
    send = jnp.concatenate([queries.transpose(1, 0, 2), attn_keys.transpose(1, 0, 2)], axis=1)
    recv = lax.all_to_all(send, "seq", split_axis=0, concat_axis=0, tiled=True)
    cond = gathered_condition(splats, splat_dest, splat_sub, splat_weight, own_blocks)
    values, recv = lax.optimization_barrier((attn_values.transpose(1, 0, 2), recv))
    values = lax.all_to_all(values, "seq", split_axis=0, concat_axis=0, tiled=True)
    probs = attention_probs(recv.reshape(peers, 2, tok_rows, head_size), 512, 128)
    cond, probs = lax.optimization_barrier((cond, probs))
    mix = jnp.dot(cond, cond_weight[:, 0], preferred_element_type=jnp.float32)
    head_out = weigh_values(probs, values, mix, 512)
    head_out = head_out.reshape(peers, tok_rows, head_size)
    arrived = lax.all_to_all(head_out, "seq", split_axis=0, concat_axis=0, tiled=True)
    return arrived.transpose(1, 0, 2)


def solution(mesh):
    in_specs = (
        P(("dp", "seq"), None, None),
        P(("dp", "seq"), None, None),
        P(("dp", "seq"), None, None),
        P(("dp", "seq"), None, None),
        P(("dp", "seq")),
        P(("dp", "seq")),
        P(("dp", "seq")),
        P(None, "seq", None),
    )
    out_specs = P(("dp", "seq"), None, None)
    return jax.shard_map(
        on_device, mesh=mesh, in_specs=in_specs, out_specs=out_specs, check_vma=False
    )
```

```python
import math

import jax
import jax.numpy as jnp
from jax import lax
from jax.experimental import pallas as pl
from jax.experimental.pallas import tpu as pltpu
from jax.sharding import PartitionSpec as P


def attention_probs(recv, tile, sub_rows):
    peers, _, rows, hd = recv.shape
    tokens = peers * rows
    to_exp2 = hd**-0.5 * math.log2(math.e)

    def kernel(q_ref, k_ref, p_ref):
        keys = k_ref[...].reshape(tokens, hd)
        for at in range(tile // sub_rows):
            q = q_ref[(at * sub_rows) // rows, 0, pl.ds((at * sub_rows) % rows, sub_rows)]
            scores = lax.dot_general(
                q, keys, (((1,), (1,)), ((), ())), preferred_element_type=jnp.float32
            )
            top = jnp.max(scores, axis=1, keepdims=True)
            probs = jnp.exp2((scores - top) * to_exp2)
            total = jnp.sum(probs, axis=1, keepdims=True)
            p_ref[pl.ds(at * sub_rows, sub_rows)] = (probs * (1.0 / total)).astype(jnp.bfloat16)

    return pl.pallas_call(
        kernel,
        name="probs",
        grid=(tokens // tile,),
        in_specs=[
            pl.BlockSpec((tile // rows, 1, rows, hd), lambda i: (i, 0, 0, 0)),
            pl.BlockSpec((peers, 1, rows, hd), lambda i: (0, 1, 0, 0)),
        ],
        out_specs=pl.BlockSpec((tile, tokens), lambda i: (i, 0)),
        out_shape=jax.ShapeDtypeStruct((tokens, tokens), jnp.bfloat16),
        cost_estimate=pl.CostEstimate(
            flops=2 * tokens * tokens * hd,
            transcendentals=tokens * tokens,
            bytes_accessed=2 * tokens * tokens,
        ),
        compiler_params=pltpu.CompilerParams(vmem_limit_bytes=24 << 20),
    )(recv, recv)


def weigh_values(probs, values, tile):
    peers, rows, hd = values.shape
    tokens = peers * rows

    def kernel(p_ref, v_ref, o_ref):
        v = v_ref[...].reshape(tokens, hd)
        o_ref[...] = jnp.dot(p_ref[...], v, preferred_element_type=jnp.float32).astype(
            jnp.bfloat16
        )

    return pl.pallas_call(
        kernel,
        name="weigh",
        grid=(tokens // tile,),
        in_specs=[
            pl.BlockSpec((tile, tokens), lambda i: (i, 0)),
            pl.BlockSpec((peers, rows, hd), lambda i: (0, 0, 0)),
        ],
        out_specs=pl.BlockSpec((tile, hd), lambda i: (i, 0)),
        out_shape=jax.ShapeDtypeStruct((tokens, hd), jnp.bfloat16),
        compiler_params=pltpu.CompilerParams(vmem_limit_bytes=24 << 20),
    )(probs, values)


def block_table(dest_ref, sub_ref, weight_ref, own_blocks, blocks):
    target = dest_ref[...] * own_blocks + sub_ref[...]
    count = target.shape[1]
    rows = lax.broadcasted_iota(jnp.int32, (blocks, count), 0)
    weight = jnp.broadcast_to(weight_ref[...].astype(jnp.float32), (blocks, count))
    return jnp.where(rows == target, weight, 0.0)


def block_sums(splats, splat_dest, splat_sub, splat_weight, own_blocks):
    peers = lax.axis_size("seq")
    count, blk_rows, feats = splats.shape
    blocks = peers * own_blocks
    half = blk_rows // 2
    core = (lax.axis_index("seq") % 2).astype(jnp.int32)[None]
    ids = [splat_dest[None], splat_sub[None], splat_weight[None]]
    id_specs = [pl.BlockSpec((1, count), lambda i, c: (0, 0)) for _ in ids]

    def pack(core_ref, dest_ref, sub_ref, weight_ref, rows_ref, out_ref):
        out_ref[: count * half] = rows_ref[...].reshape(count * half, feats)
        table = block_table(dest_ref, sub_ref, weight_ref, own_blocks, blocks)
        out_ref[count * half :] = table.T.astype(jnp.bfloat16)

    packed = pl.pallas_call(
        pack,
        name="pack_splats",
        grid_spec=pltpu.PrefetchScalarGridSpec(
            num_scalar_prefetch=1,
            grid=(1,),
            in_specs=[
                *id_specs,
                pl.BlockSpec((count, half, feats), lambda i, c: (0, 1 - c[0], 0)),
            ],
            out_specs=pl.BlockSpec((count * (half + 1), blocks), lambda i, c: (0, 0)),
        ),
        out_shape=jax.ShapeDtypeStruct((count * (half + 1), blocks), jnp.bfloat16),
    )(core, *ids, splats)
    arrived = lax.ppermute(packed, "seq", [(d, d ^ 1) for d in range(peers)])

    def sums(core_ref, dest_ref, sub_ref, weight_ref, rows_ref, other_ref, out_ref):
        table = block_table(dest_ref, sub_ref, weight_ref, own_blocks, blocks)
        other = other_ref[count * half :].astype(jnp.float32).T
        both = jnp.concatenate([table, other], axis=1)
        weight = jnp.sum(both, axis=1, keepdims=True)
        both = both.astype(jnp.bfloat16)
        mine = rows_ref[...].reshape(count, half * feats)
        theirs = other_ref[: count * half].reshape(count, half * feats)
        rows = jnp.concatenate([mine, theirs], axis=0)
        out_ref[:, : half * feats] = jnp.dot(both, rows, preferred_element_type=jnp.float32)
        out_ref[:, half * feats :] = jnp.broadcast_to(weight, (blocks, 2 * feats))

    width = (half + 2) * feats
    return pl.pallas_call(
        sums,
        name="block_sums",
        grid_spec=pltpu.PrefetchScalarGridSpec(
            num_scalar_prefetch=1,
            grid=(1,),
            in_specs=[
                *id_specs,
                pl.BlockSpec((count, half, feats), lambda i, c: (0, c[0], 0)),
                pl.BlockSpec((count * (half + 1), blocks), lambda i, c: (0, 0)),
            ],
            out_specs=pl.BlockSpec((blocks, width), lambda i, c: (0, 0)),
        ),
        out_shape=jax.ShapeDtypeStruct((blocks, width), jnp.float32),
    )(core, *ids, splats, arrived)


def own_condition(total, half, feats, own_blocks, swap):
    first_core = lax.axis_index("seq") % 2 == 0
    denom = jnp.maximum(total[:, half * feats : half * feats + 1], 1.0)
    cond = (total[:, : half * feats] / denom).astype(jnp.bfloat16)
    cond = cond.reshape(2, own_blocks, half, feats)
    mine = jnp.where(first_core, cond[0], cond[1])
    theirs = lax.ppermute(jnp.where(first_core, cond[1], cond[0]), "seq", swap)
    low = jnp.where(first_core, mine, theirs)
    high = jnp.where(first_core, theirs, mine)
    return jnp.concatenate([low, high], axis=1).reshape(own_blocks * 2 * half, feats)


def mix_values(cond, weights, values):
    heads, rows, hd = values.shape
    feats = cond.shape[1]
    group = 8

    def kernel(c_ref, w_ref, v_ref, o_ref):
        for h in range(group):
            mix = jnp.dot(c_ref[...], w_ref[h], preferred_element_type=jnp.float32)
            o_ref[h] = (v_ref[h].astype(jnp.float32) + mix).astype(jnp.bfloat16)

    return pl.pallas_call(
        kernel,
        name="mix",
        grid=(heads // group,),
        in_specs=[
            pl.BlockSpec((rows, feats), lambda i: (0, 0)),
            pl.BlockSpec((group, feats, hd), lambda i: (i, 0, 0)),
            pl.BlockSpec((group, rows, hd), lambda i: (i, 0, 0)),
        ],
        out_specs=pl.BlockSpec((group, rows, hd), lambda i: (i, 0, 0)),
        out_shape=jax.ShapeDtypeStruct((heads, rows, hd), jnp.bfloat16),
    )(cond, weights, values)


def on_device(
    queries, attn_keys, attn_values, splats, splat_dest, splat_sub, splat_weight, cond_weight
):
    tok_rows, head_count, head_size = queries.shape
    peers = lax.axis_size("seq")
    _, blk_rows, feats = splats.shape
    own_blocks = tok_rows // blk_rows
    swap = [(d, d ^ 1) for d in range(peers)]
    same_core = [[d for d in range(c, peers, 2)] for c in range(2)]
    first_core = lax.axis_index("seq") % 2 == 0

    partial = block_sums(splats, splat_dest, splat_sub, splat_weight, own_blocks)
    send = jnp.concatenate([queries.transpose(1, 0, 2), attn_keys.transpose(1, 0, 2)], axis=1)
    total = lax.psum_scatter(
        partial, "seq", scatter_dimension=0, tiled=True, axis_index_groups=same_core
    )
    recv = lax.all_to_all(send, "seq", split_axis=0, concat_axis=0, tiled=True)

    weights, _ = lax.optimization_barrier((cond_weight[:, 0], partial))
    weights = lax.all_gather(weights, "seq", axis=0, axis_index_groups=same_core)
    others = lax.ppermute(weights, "seq", swap)
    even = jnp.where(first_core, weights, others)
    odd = jnp.where(first_core, others, weights)
    weights = jnp.stack([even, odd], axis=1).reshape(head_count, feats, head_size)

    cond = own_condition(total, blk_rows // 2, feats, own_blocks, swap)
    mixed = mix_values(cond, weights, attn_values.transpose(1, 0, 2))
    mixed, recv = lax.optimization_barrier((mixed, recv))
    values = lax.all_to_all(mixed, "seq", split_axis=0, concat_axis=0, tiled=True)
    probs = attention_probs(recv.reshape(peers, 2, tok_rows, head_size), 512, 128)
    head_out = weigh_values(probs, values, 512)
    head_out = head_out.reshape(peers, tok_rows, head_size)
    arrived = lax.all_to_all(head_out, "seq", split_axis=0, concat_axis=0, tiled=True)
    return arrived.transpose(1, 0, 2)


def solution(mesh):
    in_specs = (
        P(("dp", "seq"), None, None),
        P(("dp", "seq"), None, None),
        P(("dp", "seq"), None, None),
        P(("dp", "seq"), None, None),
        P(("dp", "seq")),
        P(("dp", "seq")),
        P(("dp", "seq")),
        P(None, "seq", None),
    )
    out_specs = P(("dp", "seq"), None, None)
    return jax.shard_map(
        on_device, mesh=mesh, in_specs=in_specs, out_specs=out_specs, check_vma=False
    )
```

```python
import math

import jax
import jax.numpy as jnp
from jax import lax
from jax.experimental import pallas as pl
from jax.experimental.pallas import tpu as pltpu
from jax.sharding import PartitionSpec as P


def attention_probs(recv, tile, sub_rows):
    peers, _, rows, hd = recv.shape
    tokens = peers * rows
    to_exp2 = hd**-0.5 * math.log2(math.e)

    def kernel(q_ref, k_ref, p_ref):
        keys = k_ref[...].reshape(tokens, hd)
        for at in range(tile // sub_rows):
            q = q_ref[(at * sub_rows) // rows, 0, pl.ds((at * sub_rows) % rows, sub_rows)]
            scores = lax.dot_general(
                q, keys, (((1,), (1,)), ((), ())), preferred_element_type=jnp.float32
            )
            top = jnp.max(scores, axis=1, keepdims=True)
            probs = jnp.exp2((scores - top) * to_exp2)
            total = jnp.sum(probs, axis=1, keepdims=True)
            p_ref[pl.ds(at * sub_rows, sub_rows)] = (probs * (1.0 / total)).astype(jnp.bfloat16)

    return pl.pallas_call(
        kernel,
        name="probs",
        grid=(tokens // tile,),
        in_specs=[
            pl.BlockSpec((tile // rows, 1, rows, hd), lambda i: (i, 0, 0, 0)),
            pl.BlockSpec((peers, 1, rows, hd), lambda i: (0, 1, 0, 0)),
        ],
        out_specs=pl.BlockSpec((tile, tokens), lambda i: (i, 0)),
        out_shape=jax.ShapeDtypeStruct((tokens, tokens), jnp.bfloat16),
        cost_estimate=pl.CostEstimate(
            flops=2 * tokens * tokens * hd,
            transcendentals=tokens * tokens,
            bytes_accessed=2 * tokens * tokens,
        ),
        compiler_params=pltpu.CompilerParams(vmem_limit_bytes=24 << 20),
    )(recv, recv)


def weigh_values(probs, values, tile):
    peers, rows, hd = values.shape
    tokens = peers * rows

    def kernel(p_ref, v_ref, o_ref):
        v = v_ref[...].reshape(tokens, hd)
        o_ref[...] = jnp.dot(p_ref[...], v, preferred_element_type=jnp.float32).astype(
            jnp.bfloat16
        )

    return pl.pallas_call(
        kernel,
        name="weigh",
        grid=(tokens // tile,),
        in_specs=[
            pl.BlockSpec((tile, tokens), lambda i: (i, 0)),
            pl.BlockSpec((peers, rows, hd), lambda i: (0, 0, 0)),
        ],
        out_specs=pl.BlockSpec((tile, hd), lambda i: (i, 0)),
        out_shape=jax.ShapeDtypeStruct((tokens, hd), jnp.bfloat16),
        compiler_params=pltpu.CompilerParams(vmem_limit_bytes=24 << 20),
    )(probs, values)


def block_table(dest_ref, sub_ref, weight_ref, own_blocks, blocks):
    target = dest_ref[...] * own_blocks + sub_ref[...]
    count = target.shape[1]
    rows = lax.broadcasted_iota(jnp.int32, (blocks, count), 0)
    weight = jnp.broadcast_to(weight_ref[...].astype(jnp.float32), (blocks, count))
    return jnp.where(rows == target, weight, 0.0)


def block_sums(splats, splat_dest, splat_sub, splat_weight, own_blocks):
    peers = lax.axis_size("seq")
    count, blk_rows, feats = splats.shape
    blocks = peers * own_blocks
    half = blk_rows // 2
    core = (lax.axis_index("seq") % 2).astype(jnp.int32)[None]
    ids = [splat_dest[None], splat_sub[None], splat_weight[None]]
    id_specs = [pl.BlockSpec((1, count), lambda i, c: (0, 0)) for _ in ids]

    def pack(core_ref, dest_ref, sub_ref, weight_ref, rows_ref, out_ref):
        out_ref[: count * half] = rows_ref[...].reshape(count * half, feats)
        table = block_table(dest_ref, sub_ref, weight_ref, own_blocks, blocks)
        out_ref[count * half :] = table.T.astype(jnp.bfloat16)

    packed = pl.pallas_call(
        pack,
        name="pack_splats",
        grid_spec=pltpu.PrefetchScalarGridSpec(
            num_scalar_prefetch=1,
            grid=(1,),
            in_specs=[
                *id_specs,
                pl.BlockSpec((count, half, feats), lambda i, c: (0, 1 - c[0], 0)),
            ],
            out_specs=pl.BlockSpec((count * (half + 1), blocks), lambda i, c: (0, 0)),
        ),
        out_shape=jax.ShapeDtypeStruct((count * (half + 1), blocks), jnp.bfloat16),
    )(core, *ids, splats)
    arrived = lax.ppermute(packed, "seq", [(d, d ^ 1) for d in range(peers)])

    def sums(core_ref, dest_ref, sub_ref, weight_ref, rows_ref, other_ref, out_ref):
        table = block_table(dest_ref, sub_ref, weight_ref, own_blocks, blocks)
        other = other_ref[count * half :].astype(jnp.float32).T
        both = jnp.concatenate([table, other], axis=1)
        weight = jnp.sum(both, axis=1, keepdims=True)
        both = both.astype(jnp.bfloat16)
        mine = rows_ref[...].reshape(count, half * feats)
        theirs = other_ref[: count * half].reshape(count, half * feats)
        rows = jnp.concatenate([mine, theirs], axis=0)
        out_ref[:, : half * feats] = jnp.dot(both, rows, preferred_element_type=jnp.float32)
        out_ref[:, half * feats :] = jnp.broadcast_to(weight, (blocks, 2 * feats))

    width = (half + 2) * feats
    return pl.pallas_call(
        sums,
        name="block_sums",
        grid_spec=pltpu.PrefetchScalarGridSpec(
            num_scalar_prefetch=1,
            grid=(1,),
            in_specs=[
                *id_specs,
                pl.BlockSpec((count, half, feats), lambda i, c: (0, c[0], 0)),
                pl.BlockSpec((count * (half + 1), blocks), lambda i, c: (0, 0)),
            ],
            out_specs=pl.BlockSpec((blocks, width), lambda i, c: (0, 0)),
        ),
        out_shape=jax.ShapeDtypeStruct((blocks, width), jnp.float32),
    )(core, *ids, splats, arrived)


def own_condition(total, half, feats, own_blocks, swap):
    first_core = lax.axis_index("seq") % 2 == 0
    denom = jnp.maximum(total[:, half * feats : half * feats + 1], 1.0)
    cond = (total[:, : half * feats] / denom).astype(jnp.bfloat16)
    cond = cond.reshape(2, own_blocks, half, feats)
    mine = jnp.where(first_core, cond[0], cond[1])
    theirs = lax.ppermute(jnp.where(first_core, cond[1], cond[0]), "seq", swap)
    low = jnp.where(first_core, mine, theirs)
    high = jnp.where(first_core, theirs, mine)
    return jnp.concatenate([low, high], axis=1).reshape(own_blocks * 2 * half, feats)


def ring_gather(block, chips):
    ahead = [(2 * z + c, 2 * ((z + 1) % chips) + c) for z in range(chips) for c in range(2)]
    back = [(dst, src) for src, dst in ahead]
    found = {0: block}
    up = down = block
    for step in range(1, chips // 2 + 1):
        up = lax.ppermute(up, "seq", ahead)
        found[step] = up
        if step < chips // 2:
            down = lax.ppermute(down, "seq", back)
            found[chips - step] = down
    return jnp.stack([found[s] for s in range(chips)])


def mix_values(cond, weights, others, values):
    heads, rows, hd = values.shape
    chips, feats, _ = weights.shape
    group = 8
    place = lax.axis_index("seq").astype(jnp.int32)[None]

    def kernel(place_ref, c_ref, w_ref, w2_ref, v_ref, o_ref):
        chip, core = place_ref[0] // 2, place_ref[0] % 2
        for h in range(group):
            at = pl.program_id(0) * (group // 2) + h // 2
            at = (chip - at + chips) % chips
            w = jnp.where(core == h % 2, w_ref[at], w2_ref[at])
            mix = jnp.dot(c_ref[...], w, preferred_element_type=jnp.float32)
            o_ref[h] = (v_ref[h].astype(jnp.float32) + mix).astype(jnp.bfloat16)

    whole = pl.BlockSpec((chips, feats, hd), lambda i, p: (0, 0, 0))
    return pl.pallas_call(
        kernel,
        name="mix",
        grid_spec=pltpu.PrefetchScalarGridSpec(
            num_scalar_prefetch=1,
            grid=(heads // group,),
            in_specs=[
                pl.BlockSpec((rows, feats), lambda i, p: (0, 0)),
                whole,
                whole,
                pl.BlockSpec((group, rows, hd), lambda i, p: (i, 0, 0)),
            ],
            out_specs=pl.BlockSpec((group, rows, hd), lambda i, p: (i, 0, 0)),
        ),
        out_shape=jax.ShapeDtypeStruct((heads, rows, hd), jnp.bfloat16),
    )(place, cond, weights, others, values)


def on_device(
    queries, attn_keys, attn_values, splats, splat_dest, splat_sub, splat_weight, cond_weight
):
    tok_rows, head_count, head_size = queries.shape
    peers = lax.axis_size("seq")
    _, blk_rows, feats = splats.shape
    own_blocks = tok_rows // blk_rows
    swap = [(d, d ^ 1) for d in range(peers)]
    same_core = [[d for d in range(c, peers, 2)] for c in range(2)]

    partial = block_sums(splats, splat_dest, splat_sub, splat_weight, own_blocks)
    send = jnp.concatenate([queries.transpose(1, 0, 2), attn_keys.transpose(1, 0, 2)], axis=1)
    total = lax.psum_scatter(
        partial, "seq", scatter_dimension=0, tiled=True, axis_index_groups=same_core
    )
    recv = lax.all_to_all(send, "seq", split_axis=0, concat_axis=0, tiled=True)

    own_weights, _ = lax.optimization_barrier((cond_weight[:, 0], partial))
    weights = ring_gather(own_weights, peers // 2)
    others = lax.ppermute(weights, "seq", swap)
    cond = own_condition(total, blk_rows // 2, feats, own_blocks, swap)
    mixed = mix_values(cond, weights, others, attn_values.transpose(1, 0, 2))
    mixed, recv = lax.optimization_barrier((mixed, recv))
    values = lax.all_to_all(mixed, "seq", split_axis=0, concat_axis=0, tiled=True)
    probs = attention_probs(recv.reshape(peers, 2, tok_rows, head_size), 512, 128)
    head_out = weigh_values(probs, values, 1024)
    head_out = head_out.reshape(peers, tok_rows, head_size)
    arrived = lax.all_to_all(head_out, "seq", split_axis=0, concat_axis=0, tiled=True)
    return arrived.transpose(1, 0, 2)


def solution(mesh):
    in_specs = (
        P(("dp", "seq"), None, None),
        P(("dp", "seq"), None, None),
        P(("dp", "seq"), None, None),
        P(("dp", "seq"), None, None),
        P(("dp", "seq")),
        P(("dp", "seq")),
        P(("dp", "seq")),
        P(None, "seq", None),
    )
    out_specs = P(("dp", "seq"), None, None)
    return jax.shard_map(
        on_device, mesh=mesh, in_specs=in_specs, out_specs=out_specs, check_vma=False
    )
```

```python
import math

import jax
import jax.numpy as jnp
from jax import lax
from jax.experimental import pallas as pl
from jax.experimental.pallas import tpu as pltpu
from jax.sharding import PartitionSpec as P


def attention_probs(recv, rows, tile, sub_rows):
    peers, _, hd = recv.shape
    tokens = peers * rows
    to_exp2 = hd**-0.5 * math.log2(math.e)

    def kernel(q_ref, k_ref, p_ref):
        keys = k_ref[...].reshape(tokens, hd)
        for at in range(tile // sub_rows):
            q = q_ref[(at * sub_rows) // rows, pl.ds((at * sub_rows) % rows, sub_rows)]
            scores = lax.dot_general(
                q, keys, (((1,), (1,)), ((), ())), preferred_element_type=jnp.float32
            )
            top = jnp.max(scores, axis=1, keepdims=True)
            probs = jnp.exp2((scores - top) * to_exp2)
            total = jnp.sum(probs, axis=1, keepdims=True)
            p_ref[pl.ds(at * sub_rows, sub_rows)] = (probs * (1.0 / total)).astype(jnp.bfloat16)

    return pl.pallas_call(
        kernel,
        name="probs",
        grid=(tokens // tile,),
        in_specs=[
            pl.BlockSpec((tile // rows, rows, hd), lambda i: (i, 0, 0)),
            pl.BlockSpec((peers, rows, hd), lambda i: (0, 1, 0)),
        ],
        out_specs=pl.BlockSpec((tile, tokens), lambda i: (i, 0)),
        out_shape=jax.ShapeDtypeStruct((tokens, tokens), jnp.bfloat16),
        cost_estimate=pl.CostEstimate(
            flops=2 * tokens * tokens * hd,
            transcendentals=tokens * tokens,
            bytes_accessed=2 * tokens * tokens,
        ),
        compiler_params=pltpu.CompilerParams(vmem_limit_bytes=24 << 20),
    )(recv, recv)


def weigh_values(probs, values, tile):
    peers, rows, hd = values.shape
    tokens = peers * rows

    def kernel(p_ref, v_ref, o_ref):
        v = v_ref[...].reshape(tokens, hd)
        o_ref[...] = jnp.dot(p_ref[...], v, preferred_element_type=jnp.float32).astype(
            jnp.bfloat16
        )

    return pl.pallas_call(
        kernel,
        name="weigh",
        grid=(tokens // tile,),
        in_specs=[
            pl.BlockSpec((tile, tokens), lambda i: (i, 0)),
            pl.BlockSpec((peers, rows, hd), lambda i: (0, 0, 0)),
        ],
        out_specs=pl.BlockSpec((tile, hd), lambda i: (i, 0)),
        out_shape=jax.ShapeDtypeStruct((tokens, hd), jnp.bfloat16),
        compiler_params=pltpu.CompilerParams(vmem_limit_bytes=24 << 20),
    )(probs, values)


SLOTS = 2
KEY_ROWS = 16


def pack_slots(splats, splat_dest, splat_sub, splat_weight, peers):
    count, blk_rows, feats = splats.shape
    out_rows = SLOTS * blk_rows + KEY_ROWS

    def kernel(dest_ref, sub_ref, weight_ref, splat_ref, out_ref, which):
        for at in range(peers * SLOTS):
            which[at] = -1
        for i in range(count):
            first = dest_ref[i] * SLOTS
            which[first + (which[first] >= 0).astype(jnp.int32)] = i
        row = lax.broadcasted_iota(jnp.int32, (KEY_ROWS, feats), 0)
        lane = lax.broadcasted_iota(jnp.int32, (KEY_ROWS, feats), 1)
        for dest in range(peers):
            keys = jnp.zeros((KEY_ROWS, feats), jnp.float32)
            for slot in range(SLOTS):
                found = which[dest * SLOTS + slot]
                at = jnp.maximum(found, 0)
                out_ref[dest, slot * blk_rows : (slot + 1) * blk_rows] = splat_ref[at]
                sub = jnp.where(found >= 0, sub_ref[at], -1)
                keys = jnp.where((row == slot) & (lane == sub), weight_ref[at], keys)
            out_ref[dest, SLOTS * blk_rows :] = keys.astype(jnp.bfloat16)

    scalars = pl.BlockSpec(memory_space=pltpu.SMEM)
    return pl.pallas_call(
        kernel,
        name="pack_slots",
        in_specs=[scalars, scalars, scalars, pl.BlockSpec(memory_space=pltpu.VMEM)],
        out_specs=pl.BlockSpec(memory_space=pltpu.VMEM),
        out_shape=jax.ShapeDtypeStruct((peers, out_rows, feats), jnp.bfloat16),
        scratch_shapes=[pltpu.SMEM((peers * SLOTS,), jnp.int32)],
    )(splat_dest, splat_sub, splat_weight.astype(jnp.float32), splats)


def mix_values(recv, first_row, weights, values, own_blocks, blk_rows):
    heads, rows, hd = values.shape
    peers, _, feats = recv.shape
    group = 8
    part = KEY_ROWS
    parts = SLOTS * blk_rows // part

    def kernel(*refs):
        data_refs, key_ref = refs[:parts], refs[parts]
        w_ref, v_ref, o_ref, cond_ref = refs[parts + 1 :]

        @pl.when(pl.program_id(0) == 0)
        def _():
            sums = [[jnp.zeros((part, feats), jnp.float32)] * (blk_rows // part) for _ in range(own_blocks)]
            total = jnp.zeros((KEY_ROWS, feats), jnp.float32)
            for src in range(peers):
                keys = key_ref[src].astype(jnp.float32)
                total = total + keys
                for at in range(parts):
                    slot, piece = divmod(at * part, blk_rows)
                    data = data_refs[at][src].astype(jnp.float32)
                    for b in range(own_blocks):
                        sums[b][piece // part] += keys[slot : slot + 1, b : b + 1] * data
            weight = jnp.sum(total, axis=0, keepdims=True)
            denom = jnp.maximum(weight, 1.0)
            for b in range(own_blocks):
                for piece in range(blk_rows // part):
                    cond_ref[pl.ds(b * blk_rows + piece * part, part)] = (
                        sums[b][piece] / denom[:, b : b + 1]
                    ).astype(jnp.bfloat16)

        for h in range(group):
            mix = jnp.dot(cond_ref[...], w_ref[h], preferred_element_type=jnp.float32)
            o_ref[h] = (v_ref[h].astype(jnp.float32) + mix).astype(jnp.bfloat16)

    def piece_spec(at):
        return pl.BlockSpec((peers, part, feats), lambda i: (0, first_row // part + at, 0))

    return pl.pallas_call(
        kernel,
        name="mix",
        grid=(heads // group,),
        in_specs=[
            *[piece_spec(at) for at in range(parts + 1)],
            pl.BlockSpec((group, feats, hd), lambda i: (i, 0, 0)),
            pl.BlockSpec((group, rows, hd), lambda i: (i, 0, 0)),
        ],
        out_specs=pl.BlockSpec((group, rows, hd), lambda i: (i, 0, 0)),
        out_shape=jax.ShapeDtypeStruct((heads, rows, hd), jnp.bfloat16),
        scratch_shapes=[pltpu.VMEM((rows, feats), jnp.bfloat16)],
        compiler_params=pltpu.CompilerParams(vmem_limit_bytes=12 << 20),
    )(*[recv] * (parts + 1), weights, values)


def on_device(
    queries, attn_keys, attn_values, splats, splat_dest, splat_sub, splat_weight, cond_weight
):
    tok_rows, head_count, head_size = queries.shape
    peers = lax.axis_size("seq")
    _, blk_rows, feats = splats.shape
    own_blocks = tok_rows // blk_rows

    weights = lax.all_gather(cond_weight[:, 0], "seq", axis=0)
    slots = pack_slots(splats, splat_dest, splat_sub, splat_weight, peers)
    send = jnp.concatenate(
        [queries.transpose(1, 0, 2), attn_keys.transpose(1, 0, 2), slots], axis=1
    )
    values = attn_values.transpose(1, 0, 2)
    recv = lax.all_to_all(send, "seq", split_axis=0, concat_axis=0, tiled=True)
    values = mix_values(recv, 2 * tok_rows, weights, values, own_blocks, blk_rows)
    values = lax.all_to_all(values, "seq", split_axis=0, concat_axis=0, tiled=True)
    probs = attention_probs(recv, tok_rows, 512, 128)
    head_out = weigh_values(probs, values, 1024)
    head_out = head_out.reshape(peers, tok_rows, head_size)
    arrived = lax.all_to_all(head_out, "seq", split_axis=0, concat_axis=0, tiled=True)
    return arrived.transpose(1, 0, 2)


def solution(mesh):
    in_specs = (
        P(("dp", "seq"), None, None),
        P(("dp", "seq"), None, None),
        P(("dp", "seq"), None, None),
        P(("dp", "seq"), None, None),
        P(("dp", "seq")),
        P(("dp", "seq")),
        P(("dp", "seq")),
        P(None, "seq", None),
    )
    out_specs = P(("dp", "seq"), None, None)
    return jax.shard_map(
        on_device, mesh=mesh, in_specs=in_specs, out_specs=out_specs, check_vma=False
    )
```

```python
import math

import jax
import jax.numpy as jnp
from jax import lax
from jax.experimental import pallas as pl
from jax.experimental.pallas import tpu as pltpu
from jax.sharding import PartitionSpec as P


def attention_probs(recv, rows, tile, sub_rows):
    peers, _, hd = recv.shape
    tokens = peers * rows
    to_exp2 = hd**-0.5 * math.log2(math.e)

    def kernel(q_ref, k_ref, p_ref):
        keys = k_ref[...].reshape(tokens, hd)
        for at in range(tile // sub_rows):
            q = q_ref[(at * sub_rows) // rows, pl.ds((at * sub_rows) % rows, sub_rows)]
            scores = lax.dot_general(
                q, keys, (((1,), (1,)), ((), ())), preferred_element_type=jnp.float32
            )
            top = jnp.max(scores, axis=1, keepdims=True)
            probs = jnp.exp2((scores - top) * to_exp2)
            total = jnp.sum(probs, axis=1, keepdims=True)
            p_ref[pl.ds(at * sub_rows, sub_rows)] = (probs * (1.0 / total)).astype(jnp.bfloat16)

    return pl.pallas_call(
        kernel,
        name="probs",
        grid=(tokens // tile,),
        in_specs=[
            pl.BlockSpec((tile // rows, rows, hd), lambda i: (i, 0, 0)),
            pl.BlockSpec((peers, rows, hd), lambda i: (0, 1, 0)),
        ],
        out_specs=pl.BlockSpec((tile, tokens), lambda i: (i, 0)),
        out_shape=jax.ShapeDtypeStruct((tokens, tokens), jnp.bfloat16),
        cost_estimate=pl.CostEstimate(
            flops=2 * tokens * tokens * hd,
            transcendentals=tokens * tokens,
            bytes_accessed=2 * tokens * tokens,
        ),
        compiler_params=pltpu.CompilerParams(vmem_limit_bytes=24 << 20),
    )(recv, recv)


def weigh_values(probs, values, tile):
    peers, rows, hd = values.shape
    tokens = peers * rows

    def kernel(p_ref, v_ref, o_ref, acc_ref):
        step = pl.program_id(0)
        v = v_ref[...].reshape(tile, hd)
        part = jnp.dot(p_ref[...], v, preferred_element_type=jnp.float32)

        @pl.when(step == 0)
        def _():
            acc_ref[...] = part

        @pl.when((step > 0) & (step < pl.num_programs(0) - 1))
        def _():
            acc_ref[...] += part

        @pl.when(step == pl.num_programs(0) - 1)
        def _():
            o_ref[...] = (acc_ref[...] + part).astype(jnp.bfloat16)

    return pl.pallas_call(
        kernel,
        name="weigh",
        grid=(tokens // tile,),
        in_specs=[
            pl.BlockSpec((tokens, tile), lambda i: (0, i)),
            pl.BlockSpec((tile // rows, rows, hd), lambda i: (i, 0, 0)),
        ],
        out_specs=pl.BlockSpec((tokens, hd), lambda i: (0, 0)),
        out_shape=jax.ShapeDtypeStruct((tokens, hd), jnp.bfloat16),
        scratch_shapes=[pltpu.VMEM((tokens, hd), jnp.float32)],
        compiler_params=pltpu.CompilerParams(vmem_limit_bytes=24 << 20),
    )(probs, values)


def in_hbm(array):
    return pltpu.with_memory_space_constraint(array, pltpu.HBM)


SLOTS = 2
KEY_ROWS = 16


def pack(queries, keys, splats, splat_dest, splat_sub, splat_weight):
    rows, heads, hd = queries.shape
    count, blk_rows, feats = splats.shape
    head_rows = 2 * rows + SLOTS * blk_rows
    group = 8

    def kernel(dest_ref, sub_ref, weight_ref, q_ref, k_ref, splat_ref, out_ref, which, table):
        @pl.when(pl.program_id(0) == 0)
        def _():
            for at in range(heads * SLOTS):
                which[at] = -1
            for i in range(count):
                first = dest_ref[i] * SLOTS
                which[first + (which[first] >= 0).astype(jnp.int32)] = i
            lane = lax.broadcasted_iota(jnp.int32, (count, feats), 1)
            sub = jnp.broadcast_to(sub_ref[...], (8, count)).astype(jnp.float32).T[:, :1]
            weight = jnp.broadcast_to(weight_ref[...].astype(jnp.float32), (8, count)).T[:, :1]
            table[...] = jnp.where(lane == sub.astype(jnp.int32), weight, 0.0)

        out_ref[:, :rows] = jnp.swapaxes(q_ref[...], 0, 1)
        out_ref[:, rows : 2 * rows] = jnp.swapaxes(k_ref[...], 0, 1)
        row = lax.broadcasted_iota(jnp.int32, (KEY_ROWS, feats), 0)
        for h in range(group):
            marks = jnp.zeros((KEY_ROWS, feats), jnp.float32)
            for slot in range(SLOTS):
                found = which[(pl.program_id(0) * group + h) * SLOTS + slot]
                at = jnp.maximum(found, 0)
                to = 2 * rows + slot * blk_rows
                out_ref[h, to : to + blk_rows] = splat_ref[at]
                mark = jnp.broadcast_to(table[pl.ds(at, 1)], (KEY_ROWS, feats))
                marks = jnp.where((row == slot) & (found >= 0), mark, marks)
            out_ref[h, head_rows:] = marks.astype(jnp.bfloat16)

    by_head = pl.BlockSpec((rows, group, hd), lambda i: (0, i, 0))
    return pl.pallas_call(
        kernel,
        name="pack",
        grid=(heads // group,),
        in_specs=[
            pl.BlockSpec(memory_space=pltpu.SMEM),
            pl.BlockSpec((1, count), lambda i: (0, 0)),
            pl.BlockSpec((1, count), lambda i: (0, 0)),
            by_head,
            by_head,
            pl.BlockSpec((count, blk_rows, feats), lambda i: (0, 0, 0)),
        ],
        out_specs=pl.BlockSpec((group, head_rows + KEY_ROWS, hd), lambda i: (i, 0, 0)),
        out_shape=pltpu.HBM((heads, head_rows + KEY_ROWS, hd), jnp.bfloat16),
        scratch_shapes=[
            pltpu.SMEM((heads * SLOTS,), jnp.int32),
            pltpu.VMEM((count, feats), jnp.float32),
        ],
        compiler_params=pltpu.CompilerParams(vmem_limit_bytes=24 << 20),
    )(splat_dest, *map(in_hbm, (splat_sub[None], splat_weight[None], queries, keys, splats)))


def mix_values(recv, first_row, weights, values, own_blocks, blk_rows):
    heads, rows, hd = values.shape
    peers, _, feats = recv.shape
    group = 8
    part = KEY_ROWS
    parts = SLOTS * blk_rows // part

    def kernel(*refs):
        data_refs, key_ref = refs[:parts], refs[parts]
        w_ref, v_ref, o_ref, cond_ref = refs[parts + 1 :]

        @pl.when(pl.program_id(0) == 0)
        def _():
            sums = [[jnp.zeros((part, feats), jnp.float32)] * (blk_rows // part) for _ in range(own_blocks)]
            total = jnp.zeros((KEY_ROWS, feats), jnp.float32)
            for src in range(peers):
                keys = key_ref[src].astype(jnp.float32)
                total = total + keys
                for at in range(parts):
                    slot, piece = divmod(at * part, blk_rows)
                    data = data_refs[at][src].astype(jnp.float32)
                    for b in range(own_blocks):
                        sums[b][piece // part] += keys[slot : slot + 1, b : b + 1] * data
            weight = jnp.sum(total, axis=0, keepdims=True)
            denom = jnp.maximum(weight, 1.0)
            for b in range(own_blocks):
                for piece in range(blk_rows // part):
                    cond_ref[pl.ds(b * blk_rows + piece * part, part)] = (
                        sums[b][piece] / denom[:, b : b + 1]
                    ).astype(jnp.bfloat16)

        for h in range(group):
            mix = jnp.dot(cond_ref[...], w_ref[h], preferred_element_type=jnp.float32)
            o_ref[h] = (v_ref[h].astype(jnp.float32) + mix).astype(jnp.bfloat16)

    def piece_spec(at):
        return pl.BlockSpec((peers, part, feats), lambda i: (0, first_row // part + at, 0))

    return pl.pallas_call(
        kernel,
        name="mix",
        grid=(heads // group,),
        in_specs=[
            *[piece_spec(at) for at in range(parts + 1)],
            pl.BlockSpec((group, feats, hd), lambda i: (i, 0, 0)),
            pl.BlockSpec((group, rows, hd), lambda i: (i, 0, 0)),
        ],
        out_specs=pl.BlockSpec((group, rows, hd), lambda i: (i, 0, 0)),
        out_shape=pltpu.HBM((heads, rows, hd), jnp.bfloat16),
        scratch_shapes=[pltpu.VMEM((rows, feats), jnp.bfloat16)],
        compiler_params=pltpu.CompilerParams(vmem_limit_bytes=12 << 20),
    )(*[recv] * (parts + 1), in_hbm(weights), in_hbm(values))


def on_device(
    queries, attn_keys, attn_values, splats, splat_dest, splat_sub, splat_weight, cond_weight
):
    tok_rows, head_count, head_size = queries.shape
    peers = lax.axis_size("seq")
    _, blk_rows, feats = splats.shape
    own_blocks = tok_rows // blk_rows

    weights = lax.all_gather(cond_weight[:, 0], "seq", axis=0)
    send = pack(queries, attn_keys, splats, splat_dest, splat_sub, splat_weight)
    values = attn_values.transpose(1, 0, 2)
    recv = lax.all_to_all(send, "seq", split_axis=0, concat_axis=0, tiled=True)
    values = mix_values(recv, 2 * tok_rows, weights, values, own_blocks, blk_rows)
    values = lax.all_to_all(values, "seq", split_axis=0, concat_axis=0, tiled=True)
    probs = attention_probs(recv, tok_rows, 512, 128)
    head_out = weigh_values(probs, values, 512)
    head_out = head_out.reshape(peers, tok_rows, head_size)
    arrived = lax.all_to_all(head_out, "seq", split_axis=0, concat_axis=0, tiled=True)
    return arrived.transpose(1, 0, 2)


def solution(mesh):
    in_specs = (
        P(("dp", "seq"), None, None),
        P(("dp", "seq"), None, None),
        P(("dp", "seq"), None, None),
        P(("dp", "seq"), None, None),
        P(("dp", "seq")),
        P(("dp", "seq")),
        P(("dp", "seq")),
        P(None, "seq", None),
    )
    out_specs = P(("dp", "seq"), None, None)
    return jax.shard_map(
        on_device, mesh=mesh, in_specs=in_specs, out_specs=out_specs, check_vma=False
    )
```

```python
import math

import jax
import jax.numpy as jnp
from jax import lax
from jax.experimental import pallas as pl
from jax.experimental.pallas import tpu as pltpu
from jax.sharding import PartitionSpec as P


def attention_probs(recv, rows, tile, sub_rows):
    peers, _, hd = recv.shape
    tokens = peers * rows
    to_exp2 = hd**-0.5 * math.log2(math.e)

    def kernel(q_ref, k_ref, p_ref):
        keys = k_ref[...].reshape(tokens, hd)
        for at in range(tile // sub_rows):
            q = q_ref[(at * sub_rows) // rows, pl.ds((at * sub_rows) % rows, sub_rows)]
            scores = lax.dot_general(
                q, keys, (((1,), (1,)), ((), ())), preferred_element_type=jnp.float32
            )
            top = jnp.max(scores, axis=1, keepdims=True)
            probs = jnp.exp2((scores - top) * to_exp2)
            total = jnp.sum(probs, axis=1, keepdims=True)
            p_ref[pl.ds(at * sub_rows, sub_rows)] = (probs * (1.0 / total)).astype(jnp.bfloat16)

    return pl.pallas_call(
        kernel,
        name="probs",
        grid=(tokens // tile,),
        in_specs=[
            pl.BlockSpec((tile // rows, rows, hd), lambda i: (i, 0, 0)),
            pl.BlockSpec((peers, rows, hd), lambda i: (0, 1, 0)),
        ],
        out_specs=pl.BlockSpec((tile, tokens), lambda i: (i, 0)),
        out_shape=jax.ShapeDtypeStruct((tokens, tokens), jnp.bfloat16),
        cost_estimate=pl.CostEstimate(
            flops=2 * tokens * tokens * hd,
            transcendentals=tokens * tokens,
            bytes_accessed=2 * tokens * tokens,
        ),
        compiler_params=pltpu.CompilerParams(vmem_limit_bytes=24 << 20),
    )(recv, recv)


def weigh_values(probs, values, tile):
    peers, rows, hd = values.shape
    tokens = peers * rows

    def kernel(p_ref, v_ref, o_ref):
        v = v_ref[...].reshape(tokens, hd)
        o_ref[...] = jnp.dot(p_ref[...], v, preferred_element_type=jnp.float32).astype(
            jnp.bfloat16
        )

    return pl.pallas_call(
        kernel,
        name="weigh",
        grid=(tokens // tile,),
        in_specs=[
            pl.BlockSpec((tile, tokens), lambda i: (i, 0)),
            pl.BlockSpec((peers, rows, hd), lambda i: (0, 0, 0)),
        ],
        out_specs=pl.BlockSpec((tile, hd), lambda i: (i, 0)),
        out_shape=jax.ShapeDtypeStruct((tokens, hd), jnp.bfloat16),
        compiler_params=pltpu.CompilerParams(vmem_limit_bytes=24 << 20),
    )(probs, values)


def in_hbm(array):
    return pltpu.with_memory_space_constraint(array, pltpu.HBM)


SLOTS = 2
INFO_ROWS = 8


def splat_info(splat_dest, splat_sub, splat_weight, lanes):
    rows = jnp.stack([splat_dest.astype(jnp.bfloat16), splat_sub.astype(jnp.bfloat16), splat_weight])
    rows = jnp.pad(rows, ((0, INFO_ROWS - 3), (0, 0)))
    return jnp.pad(rows, ((0, 0), (0, lanes - splat_dest.shape[0])), constant_values=-1)


def pack(queries, keys, splats, splat_dest):
    rows, heads, hd = queries.shape
    count, blk_rows, feats = splats.shape
    out_rows = 2 * rows + SLOTS * blk_rows
    group = 8

    def kernel(dest_ref, q_ref, k_ref, splat_ref, out_ref, which):
        @pl.when(pl.program_id(0) == 0)
        def _():
            for at in range(heads * SLOTS):
                which[at] = -1
            for i in range(count):
                first = dest_ref[i] * SLOTS
                which[first + (which[first] >= 0).astype(jnp.int32)] = i

        out_ref[:, :rows] = jnp.swapaxes(q_ref[...], 0, 1)
        out_ref[:, rows : 2 * rows] = jnp.swapaxes(k_ref[...], 0, 1)
        for h in range(group):
            for slot in range(SLOTS):
                at = which[(pl.program_id(0) * group + h) * SLOTS + slot]
                to = 2 * rows + slot * blk_rows
                out_ref[h, to : to + blk_rows] = splat_ref[jnp.maximum(at, 0)]

    by_head = pl.BlockSpec((rows, group, hd), lambda i: (0, i, 0))
    return pl.pallas_call(
        kernel,
        name="pack",
        grid=(heads // group,),
        in_specs=[
            pl.BlockSpec(memory_space=pltpu.SMEM),
            by_head,
            by_head,
            pl.BlockSpec((count, blk_rows, feats), lambda i: (0, 0, 0)),
        ],
        out_specs=pl.BlockSpec((group, out_rows, hd), lambda i: (i, 0, 0)),
        out_shape=pltpu.HBM((heads, out_rows, hd), jnp.bfloat16),
        scratch_shapes=[pltpu.SMEM((heads * SLOTS,), jnp.int32)],
        compiler_params=pltpu.CompilerParams(vmem_limit_bytes=24 << 20),
    )(splat_dest, *map(in_hbm, (queries, keys, splats)))


def mix_values(recv, first_row, gathered, values, own_blocks, blk_rows):
    heads, rows, hd = values.shape
    peers, _, feats = recv.shape
    group = 8
    part = 16
    parts = SLOTS * blk_rows // part
    place = lax.axis_index("seq").astype(jnp.int32)[None]

    def slot_weights(info, own):
        dest, sub, weight = info[:, 0], info[:, 1], info[:, 2]
        mine = (dest == own).astype(jnp.float32)
        lanes = dest.shape[1]
        before = lax.broadcasted_iota(jnp.int32, (lanes, lanes), 0)
        before = (before < lax.broadcasted_iota(jnp.int32, (lanes, lanes), 1)).astype(jnp.float32)
        rank = jnp.dot(mine, before, preferred_element_type=jnp.float32)
        columns = []
        for slot in range(SLOTS):
            chosen = jnp.where((mine > 0) & (rank == slot), weight, 0.0)
            columns.append(
                [
                    jnp.sum(jnp.where(sub == b, chosen, 0.0), axis=1, keepdims=True)
                    for b in range(own_blocks)
                ]
            )
        return columns

    def kernel(place_ref, *refs):
        data_refs, info_ref = refs[:parts], refs[parts]
        w_ref, v_ref, o_ref, cond_ref = refs[parts + 1 :]

        @pl.when(pl.program_id(0) == 0)
        def _():
            own = place_ref[0].astype(jnp.float32)
            columns = slot_weights(info_ref[...].astype(jnp.float32), own)
            for b in range(own_blocks):
                weight = sum(jnp.sum(columns[slot][b], axis=0, keepdims=True) for slot in range(SLOTS))
                denom = jnp.maximum(weight, 1.0)
                for piece in range(0, blk_rows, part):
                    total = jnp.zeros((part, feats), jnp.float32)
                    for slot in range(SLOTS):
                        data_ref = data_refs[(slot * blk_rows + piece) // part]
                        scale = jnp.broadcast_to(columns[slot][b], (peers, feats))
                        data = data_ref[...].astype(jnp.float32) * scale[:, None]
                        total += jnp.sum(data, axis=0)
                    cond_ref[pl.ds(b * blk_rows + piece, part)] = (total / denom).astype(
                        jnp.bfloat16
                    )

        for h in range(group):
            mix = jnp.dot(cond_ref[...], w_ref[h], preferred_element_type=jnp.float32)
            o_ref[h] = (v_ref[h].astype(jnp.float32) + mix).astype(jnp.bfloat16)

    def piece_spec(at):
        return pl.BlockSpec((peers, part, feats), lambda i, p: (0, first_row // part + at, 0))

    return pl.pallas_call(
        kernel,
        name="mix",
        grid_spec=pltpu.PrefetchScalarGridSpec(
            num_scalar_prefetch=1,
            grid=(heads // group,),
            in_specs=[
                *[piece_spec(at) for at in range(parts)],
                pl.BlockSpec((peers, INFO_ROWS, feats), lambda i, p: (0, feats // INFO_ROWS, 0)),
                pl.BlockSpec((group, feats, hd), lambda i, p: (i, 0, 0)),
                pl.BlockSpec((group, rows, hd), lambda i, p: (i, 0, 0)),
            ],
            out_specs=pl.BlockSpec((group, rows, hd), lambda i, p: (i, 0, 0)),
            scratch_shapes=[pltpu.VMEM((rows, feats), jnp.bfloat16)],
        ),
        out_shape=pltpu.HBM((heads, rows, hd), jnp.bfloat16),
        compiler_params=pltpu.CompilerParams(vmem_limit_bytes=24 << 20),
    )(place, *[recv] * parts, *[in_hbm(gathered)] * 2, in_hbm(values))


def on_device(
    queries, attn_keys, attn_values, splats, splat_dest, splat_sub, splat_weight, cond_weight
):
    tok_rows, head_count, head_size = queries.shape
    peers = lax.axis_size("seq")
    _, blk_rows, feats = splats.shape
    own_blocks = tok_rows // blk_rows

    info = splat_info(splat_dest, splat_sub, splat_weight, feats)
    gathered = lax.all_gather(jnp.concatenate([cond_weight[:, 0], info]), "seq", axis=0)
    send = pack(queries, attn_keys, splats, splat_dest)
    values = attn_values.transpose(1, 0, 2)
    recv = lax.all_to_all(send, "seq", split_axis=0, concat_axis=0, tiled=True)
    values = mix_values(
        recv, 2 * tok_rows, gathered, values, own_blocks, blk_rows
    )
    values = lax.all_to_all(values, "seq", split_axis=0, concat_axis=0, tiled=True)
    probs = attention_probs(recv, tok_rows, 512, 128)
    head_out = weigh_values(probs, values, 1024)
    head_out = head_out.reshape(peers, tok_rows, head_size)
    arrived = lax.all_to_all(head_out, "seq", split_axis=0, concat_axis=0, tiled=True)
    return arrived.transpose(1, 0, 2)


def solution(mesh):
    in_specs = (
        P(("dp", "seq"), None, None),
        P(("dp", "seq"), None, None),
        P(("dp", "seq"), None, None),
        P(("dp", "seq"), None, None),
        P(("dp", "seq")),
        P(("dp", "seq")),
        P(("dp", "seq")),
        P(None, "seq", None),
    )
    out_specs = P(("dp", "seq"), None, None)
    return jax.shard_map(
        on_device, mesh=mesh, in_specs=in_specs, out_specs=out_specs, check_vma=False
    )
```

```python
import math

import jax
import jax.numpy as jnp
from jax import lax
from jax.experimental import pallas as pl
from jax.experimental.pallas import tpu as pltpu
from jax.sharding import PartitionSpec as P


def attention_probs(recv, rows, tile, sub_rows):
    peers, _, hd = recv.shape
    tokens = peers * rows
    to_exp2 = hd**-0.5 * math.log2(math.e)

    def kernel(q_ref, k_ref, p_ref):
        keys = k_ref[...].reshape(tokens, hd)
        for at in range(tile // sub_rows):
            q = q_ref[(at * sub_rows) // rows, pl.ds((at * sub_rows) % rows, sub_rows)]
            scores = lax.dot_general(
                q, keys, (((1,), (1,)), ((), ())), preferred_element_type=jnp.float32
            )
            top = jnp.max(scores, axis=1, keepdims=True)
            probs = jnp.exp2((scores - top) * to_exp2)
            total = jnp.sum(probs, axis=1, keepdims=True)
            p_ref[pl.ds(at * sub_rows, sub_rows)] = (probs * (1.0 / total)).astype(jnp.bfloat16)

    return pl.pallas_call(
        kernel,
        name="probs",
        grid=(tokens // tile,),
        in_specs=[
            pl.BlockSpec((tile // rows, rows, hd), lambda i: (i, 0, 0)),
            pl.BlockSpec((peers, rows, hd), lambda i: (0, 1, 0)),
        ],
        out_specs=pl.BlockSpec((tile, tokens), lambda i: (i, 0)),
        out_shape=jax.ShapeDtypeStruct((tokens, tokens), jnp.bfloat16),
        cost_estimate=pl.CostEstimate(
            flops=2 * tokens * tokens * hd,
            transcendentals=tokens * tokens,
            bytes_accessed=2 * tokens * tokens,
        ),
        compiler_params=pltpu.CompilerParams(vmem_limit_bytes=24 << 20),
    )(recv, recv)


def weigh_values(probs, values, tile, width):
    peers, rows, hd = values.shape
    tokens = peers * rows
    tiles, pieces = tokens // tile, tokens // width

    def kernel(p_ref, v_ref, o_ref, buffer, sems):
        def copy(at, piece):
            return pltpu.make_async_copy(
                p_ref.at[pl.ds(at * tile, tile), pl.ds(piece * width, width)],
                buffer.at[at % 2, piece],
                sems.at[at % 2, piece],
            )

        for at in range(2):
            for piece in range(pieces):
                copy(at, piece).start()
        for at in range(tiles):
            total = None
            for piece in range(pieces):
                copy(at, piece).wait()
                v = v_ref[piece * (width // rows) : (piece + 1) * (width // rows)]
                part = jnp.dot(
                    buffer[at % 2, piece],
                    v.reshape(width, hd),
                    preferred_element_type=jnp.float32,
                )
                total = part if total is None else total + part
                if at + 2 < tiles:
                    copy(at + 2, piece).start()
            o_ref[at * tile : (at + 1) * tile] = total.astype(jnp.bfloat16)

    return pl.pallas_call(
        kernel,
        name="weigh",
        in_specs=[
            pl.BlockSpec(memory_space=pltpu.HBM),
            pl.BlockSpec(memory_space=pltpu.VMEM),
        ],
        out_specs=pl.BlockSpec(memory_space=pltpu.VMEM),
        out_shape=jax.ShapeDtypeStruct((tokens, hd), jnp.bfloat16),
        scratch_shapes=[
            pltpu.VMEM((2, pieces, tile, width), jnp.bfloat16),
            pltpu.SemaphoreType.DMA((2, pieces)),
        ],
        compiler_params=pltpu.CompilerParams(vmem_limit_bytes=28 << 20),
    )(probs, values)


def in_hbm(array):
    return pltpu.with_memory_space_constraint(array, pltpu.HBM)


SLOTS = 2
INFO_ROWS = 8


def splat_info(splat_dest, splat_sub, splat_weight, lanes):
    rows = jnp.stack([splat_dest.astype(jnp.bfloat16), splat_sub.astype(jnp.bfloat16), splat_weight])
    rows = jnp.pad(rows, ((0, INFO_ROWS - 3), (0, 0)))
    return jnp.pad(rows, ((0, 0), (0, lanes - splat_dest.shape[0])), constant_values=-1)


def pack(queries, keys, splats, splat_dest):
    rows, heads, hd = queries.shape
    count, blk_rows, feats = splats.shape
    out_rows = 2 * rows + SLOTS * blk_rows
    group = 8

    def kernel(dest_ref, q_ref, k_ref, splat_ref, out_ref, which):
        @pl.when(pl.program_id(0) == 0)
        def _():
            for at in range(heads * SLOTS):
                which[at] = -1
            for i in range(count):
                first = dest_ref[i] * SLOTS
                which[first + (which[first] >= 0).astype(jnp.int32)] = i

        out_ref[:, :rows] = jnp.swapaxes(q_ref[...], 0, 1)
        out_ref[:, rows : 2 * rows] = jnp.swapaxes(k_ref[...], 0, 1)
        for h in range(group):
            for slot in range(SLOTS):
                at = which[(pl.program_id(0) * group + h) * SLOTS + slot]
                to = 2 * rows + slot * blk_rows
                out_ref[h, to : to + blk_rows] = splat_ref[jnp.maximum(at, 0)]

    by_head = pl.BlockSpec((rows, group, hd), lambda i: (0, i, 0))
    return pl.pallas_call(
        kernel,
        name="pack",
        grid=(heads // group,),
        in_specs=[
            pl.BlockSpec(memory_space=pltpu.SMEM),
            by_head,
            by_head,
            pl.BlockSpec((count, blk_rows, feats), lambda i: (0, 0, 0)),
        ],
        out_specs=pl.BlockSpec((group, out_rows, hd), lambda i: (i, 0, 0)),
        out_shape=pltpu.HBM((heads, out_rows, hd), jnp.bfloat16),
        scratch_shapes=[pltpu.SMEM((heads * SLOTS,), jnp.int32)],
        compiler_params=pltpu.CompilerParams(vmem_limit_bytes=24 << 20),
    )(splat_dest, *map(in_hbm, (queries, keys, splats)))


def mix_values(recv, first_row, gathered, values, own_blocks, blk_rows):
    heads, rows, hd = values.shape
    peers, _, feats = recv.shape
    group = 8
    part = 16
    parts = SLOTS * blk_rows // part
    place = lax.axis_index("seq").astype(jnp.int32)[None]

    def slot_weights(info, own):
        dest, sub, weight = info[:, 0], info[:, 1], info[:, 2]
        mine = (dest == own).astype(jnp.float32)
        lanes = dest.shape[1]
        before = lax.broadcasted_iota(jnp.int32, (lanes, lanes), 0)
        before = (before < lax.broadcasted_iota(jnp.int32, (lanes, lanes), 1)).astype(jnp.float32)
        rank = jnp.dot(mine, before, preferred_element_type=jnp.float32)
        columns = []
        for slot in range(SLOTS):
            chosen = jnp.where((mine > 0) & (rank == slot), weight, 0.0)
            columns.append(
                [
                    jnp.sum(jnp.where(sub == b, chosen, 0.0), axis=1, keepdims=True)
                    for b in range(own_blocks)
                ]
            )
        return columns

    def kernel(place_ref, *refs):
        data_refs, info_ref = refs[:parts], refs[parts]
        w_ref, v_ref, o_ref, cond_ref = refs[parts + 1 :]

        @pl.when(pl.program_id(0) == 0)
        def _():
            own = place_ref[0].astype(jnp.float32)
            columns = slot_weights(info_ref[...].astype(jnp.float32), own)
            for b in range(own_blocks):
                weight = sum(jnp.sum(columns[slot][b], axis=0, keepdims=True) for slot in range(SLOTS))
                denom = jnp.maximum(weight, 1.0)
                for piece in range(0, blk_rows, part):
                    total = jnp.zeros((part, feats), jnp.float32)
                    for slot in range(SLOTS):
                        data_ref = data_refs[(slot * blk_rows + piece) // part]
                        scale = jnp.broadcast_to(columns[slot][b], (peers, feats))
                        data = data_ref[...].astype(jnp.float32) * scale[:, None]
                        total += jnp.sum(data, axis=0)
                    cond_ref[pl.ds(b * blk_rows + piece, part)] = (total / denom).astype(
                        jnp.bfloat16
                    )

        side_by_side = jnp.concatenate([w_ref[h] for h in range(group)], axis=1)
        mix = jnp.dot(cond_ref[...], side_by_side, preferred_element_type=jnp.float32)
        for h in range(group):
            own_mix = mix[:, h * hd : (h + 1) * hd]
            o_ref[h] = (v_ref[h].astype(jnp.float32) + own_mix).astype(jnp.bfloat16)

    def piece_spec(at):
        return pl.BlockSpec((peers, part, feats), lambda i, p: (0, first_row // part + at, 0))

    return pl.pallas_call(
        kernel,
        name="mix",
        grid_spec=pltpu.PrefetchScalarGridSpec(
            num_scalar_prefetch=1,
            grid=(heads // group,),
            in_specs=[
                *[piece_spec(at) for at in range(parts)],
                pl.BlockSpec((peers, INFO_ROWS, feats), lambda i, p: (0, feats // INFO_ROWS, 0)),
                pl.BlockSpec((group, feats, hd), lambda i, p: (i, 0, 0)),
                pl.BlockSpec((group, rows, hd), lambda i, p: (i, 0, 0)),
            ],
            out_specs=pl.BlockSpec((group, rows, hd), lambda i, p: (i, 0, 0)),
            scratch_shapes=[pltpu.VMEM((rows, feats), jnp.bfloat16)],
        ),
        out_shape=pltpu.HBM((heads, rows, hd), jnp.bfloat16),
        compiler_params=pltpu.CompilerParams(vmem_limit_bytes=24 << 20),
    )(place, *[recv] * parts, *[in_hbm(gathered)] * 2, in_hbm(values))


def on_device(
    queries, attn_keys, attn_values, splats, splat_dest, splat_sub, splat_weight, cond_weight
):
    tok_rows, head_count, head_size = queries.shape
    peers = lax.axis_size("seq")
    _, blk_rows, feats = splats.shape
    own_blocks = tok_rows // blk_rows

    info = splat_info(splat_dest, splat_sub, splat_weight, feats)
    gathered = lax.all_gather(jnp.concatenate([cond_weight[:, 0], info]), "seq", axis=0)
    send = pack(queries, attn_keys, splats, splat_dest)
    values = attn_values.transpose(1, 0, 2)
    recv = lax.all_to_all(send, "seq", split_axis=0, concat_axis=0, tiled=True)
    values = mix_values(
        recv, 2 * tok_rows, gathered, values, own_blocks, blk_rows
    )
    values = lax.all_to_all(values, "seq", split_axis=0, concat_axis=0, tiled=True)
    probs = attention_probs(recv, tok_rows, 512, 128)
    head_out = weigh_values(probs, values, 1024, 1024)
    head_out = head_out.reshape(peers, tok_rows, head_size)
    arrived = lax.all_to_all(head_out, "seq", split_axis=0, concat_axis=0, tiled=True)
    return arrived.transpose(1, 0, 2)


def solution(mesh):
    in_specs = (
        P(("dp", "seq"), None, None),
        P(("dp", "seq"), None, None),
        P(("dp", "seq"), None, None),
        P(("dp", "seq"), None, None),
        P(("dp", "seq")),
        P(("dp", "seq")),
        P(("dp", "seq")),
        P(None, "seq", None),
    )
    out_specs = P(("dp", "seq"), None, None)
    return jax.shard_map(
        on_device, mesh=mesh, in_specs=in_specs, out_specs=out_specs, check_vma=False
    )
```

```python
import math

import jax
import jax.numpy as jnp
from jax import lax
from jax.experimental import pallas as pl
from jax.experimental.pallas import tpu as pltpu
from jax.sharding import PartitionSpec as P


def attention_probs(recv, rows, tile, sub_rows):
    peers, _, hd = recv.shape
    tokens = peers * rows
    to_exp2 = hd**-0.5 * math.log2(math.e)

    def kernel(q_ref, k_ref, p_ref):
        keys = k_ref[...].reshape(tokens, hd)
        for at in range(tile // sub_rows):
            q = q_ref[(at * sub_rows) // rows, pl.ds((at * sub_rows) % rows, sub_rows)]
            scores = lax.dot_general(
                q, keys, (((1,), (1,)), ((), ())), preferred_element_type=jnp.float32
            )
            top = jnp.max(scores, axis=1, keepdims=True)
            probs = jnp.exp2((scores - top) * to_exp2)
            total = jnp.sum(probs, axis=1, keepdims=True)
            p_ref[pl.ds(at * sub_rows, sub_rows)] = (probs * (1.0 / total)).astype(jnp.bfloat16)

    return pl.pallas_call(
        kernel,
        name="probs",
        grid=(tokens // tile,),
        in_specs=[
            pl.BlockSpec((tile // rows, rows, hd), lambda i: (i, 0, 0)),
            pl.BlockSpec((peers, rows, hd), lambda i: (0, 1, 0)),
        ],
        out_specs=pl.BlockSpec((tile, tokens), lambda i: (i, 0)),
        out_shape=jax.ShapeDtypeStruct((tokens, tokens), jnp.bfloat16),
        cost_estimate=pl.CostEstimate(
            flops=2 * tokens * tokens * hd,
            transcendentals=tokens * tokens,
            bytes_accessed=2 * tokens * tokens,
        ),
        compiler_params=pltpu.CompilerParams(vmem_limit_bytes=24 << 20),
    )(recv, recv)


def weigh_values(probs, values, tile):
    peers, rows, hd = values.shape
    tokens = peers * rows

    def kernel(p_ref, v_ref, o_ref):
        v = v_ref[...].reshape(tokens, hd)
        o_ref[...] = jnp.dot(p_ref[...], v, preferred_element_type=jnp.float32).astype(
            jnp.bfloat16
        )

    return pl.pallas_call(
        kernel,
        name="weigh",
        grid=(tokens // tile,),
        in_specs=[
            pl.BlockSpec((tile, tokens), lambda i: (i, 0)),
            pl.BlockSpec((peers, rows, hd), lambda i: (0, 0, 0)),
        ],
        out_specs=pl.BlockSpec((tile, hd), lambda i: (i, 0)),
        out_shape=jax.ShapeDtypeStruct((tokens, hd), jnp.bfloat16),
        compiler_params=pltpu.CompilerParams(vmem_limit_bytes=24 << 20),
    )(probs, values)


def in_hbm(array):
    return pltpu.with_memory_space_constraint(array, pltpu.HBM)


SLOTS = 2
INFO_ROWS = 8


def splat_info(splat_dest, splat_sub, splat_weight, lanes):
    rows = jnp.stack([splat_dest.astype(jnp.bfloat16), splat_sub.astype(jnp.bfloat16), splat_weight])
    rows = jnp.pad(rows, ((0, INFO_ROWS - 3), (0, 0)))
    return jnp.pad(rows, ((0, 0), (0, lanes - splat_dest.shape[0])), constant_values=-1)


def pack(queries, keys, splats, splat_dest):
    rows, heads, hd = queries.shape
    count, blk_rows, feats = splats.shape
    out_rows = 2 * rows + SLOTS * blk_rows
    group = 8

    def kernel(dest_ref, q_ref, k_ref, splat_ref, out_ref, which):
        @pl.when(pl.program_id(0) == 0)
        def _():
            for at in range(heads * SLOTS):
                which[at] = -1
            for i in range(count):
                first = dest_ref[i] * SLOTS
                which[first + (which[first] >= 0).astype(jnp.int32)] = i

        out_ref[:, :rows] = jnp.swapaxes(q_ref[...], 0, 1)
        out_ref[:, rows : 2 * rows] = jnp.swapaxes(k_ref[...], 0, 1)
        for h in range(group):
            for slot in range(SLOTS):
                at = which[(pl.program_id(0) * group + h) * SLOTS + slot]
                to = 2 * rows + slot * blk_rows
                out_ref[h, to : to + blk_rows] = splat_ref[jnp.maximum(at, 0)]

    by_head = pl.BlockSpec((rows, group, hd), lambda i: (0, i, 0))
    return pl.pallas_call(
        kernel,
        name="pack",
        grid=(heads // group,),
        in_specs=[
            pl.BlockSpec(memory_space=pltpu.SMEM),
            by_head,
            by_head,
            pl.BlockSpec((count, blk_rows, feats), lambda i: (0, 0, 0)),
        ],
        out_specs=pl.BlockSpec((group, out_rows, hd), lambda i: (i, 0, 0)),
        out_shape=pltpu.HBM((heads, out_rows, hd), jnp.bfloat16),
        scratch_shapes=[pltpu.SMEM((heads * SLOTS,), jnp.int32)],
        compiler_params=pltpu.CompilerParams(vmem_limit_bytes=24 << 20),
    )(splat_dest, *map(in_hbm, (queries, keys, splats)))


def slot_weights(info, own_blocks):
    peers, _, lanes = info.shape
    place = lax.axis_index("seq").astype(jnp.int32)[None]

    def kernel(place_ref, info_ref, scale_ref, denom_ref):
        rows = info_ref[...].astype(jnp.float32)
        dest, sub, weight = rows[:, 0], rows[:, 1], rows[:, 2]
        mine = (dest == place_ref[0].astype(jnp.float32)).astype(jnp.float32)
        before = lax.broadcasted_iota(jnp.int32, (lanes, lanes), 0)
        before = (before < lax.broadcasted_iota(jnp.int32, (lanes, lanes), 1)).astype(jnp.float32)
        rank = jnp.dot(mine, before, preferred_element_type=jnp.float32)
        for b in range(own_blocks):
            total = jnp.zeros((1, lanes), jnp.float32)
            for slot in range(SLOTS):
                chosen = (mine > 0) & (rank == slot) & (sub == b)
                column = jnp.sum(jnp.where(chosen, weight, 0.0), axis=1, keepdims=True)
                scale = jnp.broadcast_to(column, (peers, lanes))
                scale_ref[slot * own_blocks + b] = scale
                total += jnp.sum(scale, axis=0, keepdims=True)
            denom_ref[b] = jnp.broadcast_to(jnp.maximum(total, 1.0), (8, lanes))

    return pl.pallas_call(
        kernel,
        name="slot_weights",
        in_specs=[
            pl.BlockSpec(memory_space=pltpu.SMEM),
            pl.BlockSpec(memory_space=pltpu.VMEM),
        ],
        out_specs=[pl.BlockSpec(memory_space=pltpu.VMEM)] * 2,
        out_shape=[
            pltpu.HBM((SLOTS * own_blocks, peers, lanes), jnp.float32),
            pltpu.HBM((own_blocks, 8, lanes), jnp.float32),
        ],
    )(place, info)


def mix_values(recv, first_row, gathered, values, own_blocks, blk_rows):
    heads, rows, hd = values.shape
    peers, _, feats = recv.shape
    group = 16
    part = 16
    parts = SLOTS * blk_rows // part
    scales, denoms = slot_weights(gathered[:, feats:], own_blocks)

    def kernel(*refs):
        data_refs = refs[:parts]
        scale_ref, denom_ref, w_ref, v_ref, o_ref, cond_ref = refs[parts:]

        @pl.when(pl.program_id(0) == 0)
        def _():
            for piece in range(0, blk_rows, part):
                total = [jnp.zeros((part, feats), jnp.float32) for _ in range(own_blocks)]
                for slot in range(SLOTS):
                    data_ref = data_refs[(slot * blk_rows + piece) // part]
                    for src in range(peers):
                        data = data_ref[src].astype(jnp.float32)
                        for b in range(own_blocks):
                            scale = scale_ref[slot * own_blocks + b, pl.ds(src, 1)]
                            total[b] += data * scale
                for b in range(own_blocks):
                    cond_ref[pl.ds(b * blk_rows + piece, part)] = (
                        total[b] / denom_ref[b, :1]
                    ).astype(jnp.bfloat16)

        side_by_side = jnp.concatenate([w_ref[h] for h in range(group)], axis=1)
        mix = jnp.dot(cond_ref[...], side_by_side, preferred_element_type=jnp.float32)
        for h in range(group):
            own_mix = mix[:, h * hd : (h + 1) * hd]
            o_ref[h] = (v_ref[h].astype(jnp.float32) + own_mix).astype(jnp.bfloat16)

    def piece_spec(at):
        return pl.BlockSpec((peers, part, feats), lambda i: (0, first_row // part + at, 0))

    return pl.pallas_call(
        kernel,
        name="mix",
        grid=(heads // group,),
        in_specs=[
            *[piece_spec(at) for at in range(parts)],
            pl.BlockSpec((SLOTS * own_blocks, peers, feats), lambda i: (0, 0, 0)),
            pl.BlockSpec((own_blocks, 8, feats), lambda i: (0, 0, 0)),
            pl.BlockSpec((group, feats, hd), lambda i: (i, 0, 0)),
            pl.BlockSpec((group, rows, hd), lambda i: (i, 0, 0)),
        ],
        out_specs=pl.BlockSpec((group, rows, hd), lambda i: (i, 0, 0)),
        out_shape=pltpu.HBM((heads, rows, hd), jnp.bfloat16),
        scratch_shapes=[pltpu.VMEM((rows, feats), jnp.bfloat16)],
        compiler_params=pltpu.CompilerParams(vmem_limit_bytes=24 << 20),
    )(*[recv] * parts, *map(in_hbm, (scales, denoms, gathered, values)))


def on_device(
    queries, attn_keys, attn_values, splats, splat_dest, splat_sub, splat_weight, cond_weight
):
    tok_rows, head_count, head_size = queries.shape
    peers = lax.axis_size("seq")
    _, blk_rows, feats = splats.shape
    own_blocks = tok_rows // blk_rows

    info = splat_info(splat_dest, splat_sub, splat_weight, feats)
    gathered = lax.all_gather(jnp.concatenate([cond_weight[:, 0], info]), "seq", axis=0)
    send = pack(queries, attn_keys, splats, splat_dest)
    values = attn_values.transpose(1, 0, 2)
    recv = lax.all_to_all(send, "seq", split_axis=0, concat_axis=0, tiled=True)
    values = mix_values(
        recv, 2 * tok_rows, gathered, values, own_blocks, blk_rows
    )
    values = lax.all_to_all(values, "seq", split_axis=0, concat_axis=0, tiled=True)
    probs = attention_probs(recv, tok_rows, 512, 128)
    head_out = weigh_values(probs, values, 1024)
    head_out = head_out.reshape(peers, tok_rows, head_size)
    arrived = lax.all_to_all(head_out, "seq", split_axis=0, concat_axis=0, tiled=True)
    return arrived.transpose(1, 0, 2)


def solution(mesh):
    in_specs = (
        P(("dp", "seq"), None, None),
        P(("dp", "seq"), None, None),
        P(("dp", "seq"), None, None),
        P(("dp", "seq"), None, None),
        P(("dp", "seq")),
        P(("dp", "seq")),
        P(("dp", "seq")),
        P(None, "seq", None),
    )
    out_specs = P(("dp", "seq"), None, None)
    return jax.shard_map(
        on_device, mesh=mesh, in_specs=in_specs, out_specs=out_specs, check_vma=False
    )
```

```python
import math

import jax
import jax.numpy as jnp
from jax import lax
from jax.experimental import pallas as pl
from jax.experimental.pallas import tpu as pltpu
from jax.sharding import PartitionSpec as P


def attention_probs(recv, rows, tile, sub_rows):
    peers, _, hd = recv.shape
    tokens = peers * rows
    to_exp2 = hd**-0.5 * math.log2(math.e)

    def kernel(q_ref, k_ref, p_ref):
        keys = k_ref[...].reshape(tokens, hd)
        for at in range(tile // sub_rows):
            q = q_ref[(at * sub_rows) // rows, pl.ds((at * sub_rows) % rows, sub_rows)]
            scores = lax.dot_general(
                q, keys, (((1,), (1,)), ((), ())), preferred_element_type=jnp.float32
            )
            top = jnp.max(scores, axis=1, keepdims=True)
            probs = jnp.exp2((scores - top) * to_exp2)
            total = jnp.sum(probs, axis=1, keepdims=True)
            p_ref[pl.ds(at * sub_rows, sub_rows)] = (probs * (1.0 / total)).astype(jnp.bfloat16)

    return pl.pallas_call(
        kernel,
        name="probs",
        grid=(tokens // tile,),
        in_specs=[
            pl.BlockSpec((tile // rows, rows, hd), lambda i: (i, 0, 0)),
            pl.BlockSpec((peers, rows, hd), lambda i: (0, 1, 0)),
        ],
        out_specs=pl.BlockSpec((tile, tokens), lambda i: (i, 0)),
        out_shape=jax.ShapeDtypeStruct((tokens, tokens), jnp.bfloat16),
        cost_estimate=pl.CostEstimate(
            flops=2 * tokens * tokens * hd,
            transcendentals=tokens * tokens,
            bytes_accessed=2 * tokens * tokens,
        ),
        compiler_params=pltpu.CompilerParams(vmem_limit_bytes=24 << 20),
    )(recv, recv)


def weigh_values(probs, values, tile):
    peers, rows, hd = values.shape
    tokens = peers * rows

    def kernel(p_ref, v_ref, o_ref):
        v = v_ref[...].reshape(tokens, hd)
        o_ref[...] = jnp.dot(p_ref[...], v, preferred_element_type=jnp.float32).astype(
            jnp.bfloat16
        )

    return pl.pallas_call(
        kernel,
        name="weigh",
        grid=(tokens // tile,),
        in_specs=[
            pl.BlockSpec((tile, tokens), lambda i: (i, 0)),
            pl.BlockSpec((peers, rows, hd), lambda i: (0, 0, 0)),
        ],
        out_specs=pl.BlockSpec((tile, hd), lambda i: (i, 0)),
        out_shape=jax.ShapeDtypeStruct((tokens, hd), jnp.bfloat16),
        compiler_params=pltpu.CompilerParams(vmem_limit_bytes=24 << 20),
    )(probs, values)


def in_hbm(array):
    return pltpu.with_memory_space_constraint(array, pltpu.HBM)


SLOTS = 2
INFO_ROWS = 8


def splat_info(splat_dest, splat_sub, splat_weight, lanes):
    rows = jnp.stack([splat_dest.astype(jnp.bfloat16), splat_sub.astype(jnp.bfloat16), splat_weight])
    rows = jnp.pad(rows, ((0, INFO_ROWS - 3), (0, 0)))
    return jnp.pad(rows, ((0, 0), (0, lanes - splat_dest.shape[0])), constant_values=-1)


def pack(queries, keys, splats, splat_dest):
    rows, heads, hd = queries.shape
    count, blk_rows, feats = splats.shape
    out_rows = 2 * rows + SLOTS * blk_rows
    group = 8

    def kernel(dest_ref, q_ref, k_ref, splat_ref, out_ref, which):
        @pl.when(pl.program_id(0) == 0)
        def _():
            for at in range(heads * SLOTS):
                which[at] = -1
            for i in range(count):
                first = dest_ref[i] * SLOTS
                which[first + (which[first] >= 0).astype(jnp.int32)] = i

        out_ref[:, :rows] = jnp.swapaxes(q_ref[...], 0, 1)
        out_ref[:, rows : 2 * rows] = jnp.swapaxes(k_ref[...], 0, 1)
        for h in range(group):
            for slot in range(SLOTS):
                at = which[(pl.program_id(0) * group + h) * SLOTS + slot]
                to = 2 * rows + slot * blk_rows
                out_ref[h, to : to + blk_rows] = splat_ref[jnp.maximum(at, 0)]

    by_head = pl.BlockSpec((rows, group, hd), lambda i: (0, i, 0))
    return pl.pallas_call(
        kernel,
        name="pack",
        grid=(heads // group,),
        in_specs=[
            pl.BlockSpec(memory_space=pltpu.SMEM),
            by_head,
            by_head,
            pl.BlockSpec((count, blk_rows, feats), lambda i: (0, 0, 0)),
        ],
        out_specs=pl.BlockSpec((group, out_rows, hd), lambda i: (i, 0, 0)),
        out_shape=pltpu.HBM((heads, out_rows, hd), jnp.bfloat16),
        scratch_shapes=[pltpu.SMEM((heads * SLOTS,), jnp.int32)],
        compiler_params=pltpu.CompilerParams(vmem_limit_bytes=24 << 20),
    )(*map(in_hbm, (splat_dest, queries, keys, splats)))


def slot_weights(info, own_blocks):
    peers, _, lanes = info.shape
    place = lax.axis_index("seq").astype(jnp.int32)[None]

    def kernel(place_ref, info_ref, scale_ref, denom_ref):
        rows = info_ref[...].astype(jnp.float32)
        dest, sub, weight = rows[:, 0], rows[:, 1], rows[:, 2]
        mine = (dest == place_ref[0].astype(jnp.float32)).astype(jnp.float32)
        before = lax.broadcasted_iota(jnp.int32, (lanes, lanes), 0)
        before = (before < lax.broadcasted_iota(jnp.int32, (lanes, lanes), 1)).astype(jnp.float32)
        rank = jnp.dot(mine, before, preferred_element_type=jnp.float32)
        for b in range(own_blocks):
            total = jnp.zeros((1, lanes), jnp.float32)
            for slot in range(SLOTS):
                chosen = (mine > 0) & (rank == slot) & (sub == b)
                column = jnp.sum(jnp.where(chosen, weight, 0.0), axis=1, keepdims=True)
                scale = jnp.broadcast_to(column, (peers, lanes))
                scale_ref[slot * own_blocks + b] = scale
                total += jnp.sum(scale, axis=0, keepdims=True)
            denom_ref[b] = jnp.broadcast_to(jnp.maximum(total, 1.0), (8, lanes))

    return pl.pallas_call(
        kernel,
        name="slot_weights",
        in_specs=[
            pl.BlockSpec(memory_space=pltpu.SMEM),
            pl.BlockSpec(memory_space=pltpu.VMEM),
        ],
        out_specs=[pl.BlockSpec(memory_space=pltpu.VMEM)] * 2,
        out_shape=[
            pltpu.HBM((SLOTS * own_blocks, peers, lanes), jnp.float32),
            pltpu.HBM((own_blocks, 8, lanes), jnp.float32),
        ],
    )(place, info)


def mix_values(recv, first_row, gathered, values, own_blocks, blk_rows):
    heads, rows, hd = values.shape
    peers, _, feats = recv.shape
    group = 16
    part = 16
    parts = SLOTS * blk_rows // part
    scales, denoms = slot_weights(gathered[:, feats:], own_blocks)

    def kernel(*refs):
        data_refs = refs[:parts]
        scale_ref, denom_ref, w_ref, v_ref, o_ref, cond_ref = refs[parts:]

        @pl.when(pl.program_id(0) == 0)
        def _():
            for piece in range(0, blk_rows, part):
                total = [jnp.zeros((part, feats), jnp.float32) for _ in range(own_blocks)]
                for slot in range(SLOTS):
                    data_ref = data_refs[(slot * blk_rows + piece) // part]
                    for src in range(peers):
                        data = data_ref[src].astype(jnp.float32)
                        for b in range(own_blocks):
                            scale = scale_ref[slot * own_blocks + b, pl.ds(src, 1)]
                            total[b] += data * scale
                for b in range(own_blocks):
                    cond_ref[pl.ds(b * blk_rows + piece, part)] = (
                        total[b] / denom_ref[b, :1]
                    ).astype(jnp.bfloat16)

        side_by_side = jnp.concatenate([w_ref[h] for h in range(group)], axis=1)
        mix = jnp.dot(cond_ref[...], side_by_side, preferred_element_type=jnp.float32)
        for h in range(group):
            own_mix = mix[:, h * hd : (h + 1) * hd]
            o_ref[h] = (v_ref[h].astype(jnp.float32) + own_mix).astype(jnp.bfloat16)

    def piece_spec(at):
        return pl.BlockSpec((peers, part, feats), lambda i: (0, first_row // part + at, 0))

    return pl.pallas_call(
        kernel,
        name="mix",
        grid=(heads // group,),
        in_specs=[
            *[piece_spec(at) for at in range(parts)],
            pl.BlockSpec((SLOTS * own_blocks, peers, feats), lambda i: (0, 0, 0)),
            pl.BlockSpec((own_blocks, 8, feats), lambda i: (0, 0, 0)),
            pl.BlockSpec((group, feats, hd), lambda i: (i, 0, 0)),
            pl.BlockSpec((group, rows, hd), lambda i: (i, 0, 0)),
        ],
        out_specs=pl.BlockSpec((group, rows, hd), lambda i: (i, 0, 0)),
        out_shape=pltpu.HBM((heads, rows, hd), jnp.bfloat16),
        scratch_shapes=[pltpu.VMEM((rows, feats), jnp.bfloat16)],
        compiler_params=pltpu.CompilerParams(vmem_limit_bytes=24 << 20),
    )(*[recv] * parts, *map(in_hbm, (scales, denoms, gathered, values)))


def on_device(
    queries, attn_keys, attn_values, splats, splat_dest, splat_sub, splat_weight, cond_weight
):
    tok_rows, head_count, head_size = queries.shape
    peers = lax.axis_size("seq")
    _, blk_rows, feats = splats.shape
    own_blocks = tok_rows // blk_rows

    info = splat_info(splat_dest, splat_sub, splat_weight, feats)
    gathered = lax.all_gather(jnp.concatenate([cond_weight[:, 0], info]), "seq", axis=0)
    send = pack(queries, attn_keys, splats, splat_dest)
    values = attn_values.transpose(1, 0, 2)
    recv = lax.all_to_all(send, "seq", split_axis=0, concat_axis=0, tiled=True)
    values = mix_values(
        recv, 2 * tok_rows, gathered, values, own_blocks, blk_rows
    )
    values = lax.all_to_all(values, "seq", split_axis=0, concat_axis=0, tiled=True)
    probs = attention_probs(recv, tok_rows, 512, 128)
    head_out = weigh_values(probs, values, 1024)
    head_out = head_out.reshape(peers, tok_rows, head_size)
    arrived = lax.all_to_all(head_out, "seq", split_axis=0, concat_axis=0, tiled=True)
    return arrived.transpose(1, 0, 2)


def solution(mesh):
    in_specs = (
        P(("dp", "seq"), None, None),
        P(("dp", "seq"), None, None),
        P(("dp", "seq"), None, None),
        P(("dp", "seq"), None, None),
        P(("dp", "seq")),
        P(("dp", "seq")),
        P(("dp", "seq")),
        P(None, "seq", None),
    )
    out_specs = P(("dp", "seq"), None, None)
    return jax.shard_map(
        on_device, mesh=mesh, in_specs=in_specs, out_specs=out_specs, check_vma=False
    )
```
